256 devices in a mesh: dp: 8 (over y, z_lo), seq: 32 (over x, z_hi, core).
Axes of the slice: x: 4, y: 4, z: 8 (z_hi: 4, z_lo: 2; z = z_hi * 2 + z_lo), core: 2. Of those that a mesh axis runs over, the one named last changes fastest.
Arguments:
- queries: bfloat16 [8, 4096, 2048], P('dp', 'seq'), may hold values from -6 to 6
- keys: bfloat16 [8, 4096, 2048], P('dp', 'seq'), may hold values from -6 to 6
- values: bfloat16 [8, 4096, 2048], P('dp', 'seq'), may hold values from -6 to 6
- frames: int32 [8, 4096], P('dp', 'seq'), may hold values from 0 to 340, never falling along the last dimension, each value on 1 to 16 neighbouring positions
- out_weight: bfloat16 [2048, 2048], P('seq'), may hold values from -0.125 to 0.125
- cotangent: bfloat16 [8, 4096, 2048], P('dp', 'seq'), may hold values from -6 to 6
Outputs:
- output: bfloat16 [8, 4096, 2048], P('dp', 'seq')
- grad_queries: bfloat16 [8, 4096, 2048], P('dp', 'seq')
- grad_keys: bfloat16 [8, 4096, 2048], P('dp', 'seq')
- grad_values: bfloat16 [8, 4096, 2048], P('dp', 'seq')
- grad_weight: float32 [2048, 2048], P('seq')
The draws below stay inside these ranges and needn't reach their ends.
Inputs may be any that keep to these rules, and one draw needn't show every extreme that they name: `frames`: within each clip the frame index never falls along the tokens, starts at 0, and every frame 0 to 340 holds 1 to 16 consecutive tokens; some frame holds exactly 16.
All inputs are finite; a program needn't handle non-finite values.
Results may differ from the reference program's by a relative error of at most 0.022.
Values may be sent and summed in bfloat16 or wider, within the bound.
A program may use at most 128 MiB of HBM per device.

```python
import math
from functools import partial
import jax
import jax.numpy as jnp
import numpy as np
from jax import lax

D = 2048
H = 32
HS = 64
SLOTS = 16
HD = 2048
L = 4096
CLIPS = 8
FRAMES = 341


def draw_queries(key, part):
    drawn_key = jax.random.fold_in(key, 11)
    return jnp.clip(jax.random.normal(drawn_key, (CLIPS, L, HD), jnp.float32), -4.0, 4.0).astype(jnp.bfloat16)


def draw_keys(key, part):
    drawn_key = jax.random.fold_in(key, 13)
    return jnp.clip(jax.random.normal(drawn_key, (CLIPS, L, HD), jnp.float32), -4.0, 4.0).astype(jnp.bfloat16)


def steps_of(rng, dims, shards, low, high):
    def one(position, blocks):
        heights = jax.random.uniform(jax.random.fold_in(jax.random.fold_in(rng, 6), position), (blocks,), jnp.float32, low / len(shards), high / len(shards))
        return jnp.repeat(jnp.exp(heights), dims[position] // blocks).reshape((-1,) + (1,) * (len(dims) - position - 1))

    factor_of = one(*shards[0])
    for cut in shards[1:]:
        factor_of = factor_of * one(*cut)
    return factor_of


def split_up(amount, total, reach, skew):
    portions = [(1 << 20) // math.isqrt(standing ** skew) + 1 for standing in range(2, amount + 1)]
    rest, given = total - reach - (amount - 1), [1] * (amount - 1)
    while rest > 0:
        movable = [i for i in range(amount - 1) if given[i] < reach]
        whole, left = sum([portions[i] for i in movable]), rest
        for i in movable:
            more = min(reach - given[i], max(1, left * portions[i] // whole), rest)
            given[i] = given[i] + more
            rest = rest - more
    return np.array([reach] + given)


def uneven_parts(rng, count, total, limit, slope):
    if count == 2:
        one = jax.random.randint(rng, (), max(1, total - limit), min(limit, total - 1) + 1)
        return jnp.stack([one, total - one])
    tallies = jnp.asarray(split_up(count, total, limit, slope), jnp.int32)
    pairs = (count - 1) // 2
    giver, receiver = tallies[1:1 + 2 * pairs:2], tallies[2:2 + 2 * pairs:2]
    margin = jnp.minimum(giver - 1, limit - receiver)
    passed = jax.random.randint(jax.random.fold_in(rng, 1), (pairs,), 0, 1 << 20) % (margin + 1)
    tallies = tallies.at[1:1 + 2 * pairs:2].set(giver - passed).at[2:2 + 2 * pairs:2].set(receiver + passed)
    return tallies[jax.random.permutation(jax.random.fold_in(rng, 2), count)]


def centred(key, dims, spread, bound, shards=(), kind=jnp.bfloat16):
    values = jax.random.normal(key, dims, jnp.float32) * spread
    if len(shards) > 0:
        values = steps_of(key, dims, shards, -0.22, 0.18) * values
    return jnp.clip(values, min=-bound, max=bound).astype(kind)


def setup_inputs(seed: int = 0) -> dict:
    key_of = jax.random.split(jax.random.key(seed), 7)
    return {
        "queries": draw_queries(jax.random.fold_in(key_of[6], 71), 0),
        "keys": draw_keys(jax.random.fold_in(key_of[6], 71), 0),
        "values": centred(key_of[2], (CLIPS, L, HD), 1.0, 6.0, ((0, 8), (1, 32))),
        "frames": jax.vmap(lambda own: jnp.searchsorted(jnp.cumsum(uneven_parts(own, FRAMES, L, SLOTS, 1)), jnp.arange(L), side="right"))(jax.random.split(key_of[3], CLIPS)).reshape((CLIPS, L)).astype(jnp.int32),
        "out_weight": centred(key_of[4], (HD, D), HD ** -0.5, 0.125, ((0, 32),)),
        "cotangent": centred(key_of[5], (CLIPS, L, D), 1.0, 6.0, ((0, 8), (1, 32))),
    }


def head_pass(query_head, key_head, value_head, frame_row, grad_head):
    score_scale = HS ** -0.5
    scores = jnp.dot(query_head, key_head.T, preferred_element_type=jnp.float32) * score_scale
    allowed = frame_row[None, :] <= frame_row[:, None]
    scores = jnp.where(allowed, scores, -1.0e30)
    highest = jnp.max(scores, axis=1, keepdims=True)
    exp_mass = jnp.sum(jnp.where(allowed, jnp.exp(scores - highest), 0.0), axis=1, keepdims=True)
    log_mass = highest + jnp.log(exp_mass)
    probabilities = jnp.where(allowed, jnp.exp(scores - log_mass), 0.0)
    attn_weights = probabilities.astype(jnp.bfloat16)
    attention = jnp.dot(attn_weights, value_head, preferred_element_type=jnp.float32).astype(jnp.bfloat16)
    grad_value = jnp.dot(attn_weights.T, grad_head, preferred_element_type=jnp.float32).astype(jnp.bfloat16)
    grad_probs = jnp.dot(grad_head, value_head.T, preferred_element_type=jnp.float32)
    delta_rows = jnp.sum(grad_head.astype(jnp.float32) * attention.astype(jnp.float32), axis=1, keepdims=True)
    grad_scores = (probabilities * (grad_probs - delta_rows)).astype(jnp.bfloat16)
    grad_query = (jnp.dot(grad_scores, key_head, preferred_element_type=jnp.float32) * score_scale).astype(jnp.bfloat16)
    grad_key = (jnp.dot(grad_scores.T, query_head, preferred_element_type=jnp.float32) * score_scale).astype(jnp.bfloat16)
    return attention, grad_query, grad_key, grad_value


def merge_heads(stacked):
    return jnp.transpose(stacked, (1, 0, 2)).reshape(stacked.shape[1], H * HS)


def clip_pass(out_weight, packed):
    query_clip, key_clip, value_clip, frame_row, grad_out = packed
    grad_attention = jnp.dot(grad_out, out_weight.T, preferred_element_type=jnp.float32).astype(jnp.bfloat16)

    def per_head(head_index):
        first_col = (head_index * HS).astype(jnp.int32)

        def select_head(source):
            return lax.dynamic_slice_in_dim(source, first_col, HS, 1)

        return head_pass(select_head(query_clip), select_head(key_clip), select_head(value_clip),
                         frame_row, select_head(grad_attention))

    attention, grad_query, grad_key, grad_value = lax.map(per_head, jnp.arange(H, dtype=jnp.int32))
    attention = merge_heads(attention)
    output = jnp.dot(attention, out_weight, preferred_element_type=jnp.float32).astype(jnp.bfloat16)
    weight_term = jnp.dot(attention.T, grad_out, preferred_element_type=jnp.float32)
    return output, merge_heads(grad_query), merge_heads(grad_key), merge_heads(grad_value), weight_term


def reference(queries, keys, values, frames, out_weight, cotangent):
    output, grad_queries, grad_keys, grad_values, weight_terms = lax.map(
        partial(clip_pass, out_weight), (queries, keys, values, frames, cotangent))
    grad_weight = jnp.sum(weight_terms, axis=0)
    return output, grad_queries, grad_keys, grad_values, grad_weight
```

```python
import jax
import jax.numpy as jnp
from jax import lax
from jax.experimental import pallas as pl
from jax.experimental.pallas import tpu as pltpu
from jax.sharding import PartitionSpec as P

HS = 64
QB = 512
QH = 256
KT = 512
TAIL = 16
NEG = -1e30
f32, bf = jnp.float32, jnp.bfloat16
VM = pl.BlockSpec(memory_space=pltpu.VMEM)


def dg(a, b, ca, cb):
    return lax.dot_general(a, b, (((ca,), (cb,)), ((), ())), preferred_element_type=f32)


def pack_qkv_kernel(q_ref, k_ref, v_ref, out_ref):
    tok = q_ref.shape[0]
    half = tok // 2
    for h in range(q_ref.shape[1] // HS):
        cols = slice(h * HS, (h + 1) * HS)
        out_ref[h, 0:tok, 0:HS] = q_ref[:, cols]
        out_ref[h, 0:tok, HS : 2 * HS] = k_ref[:, cols]
        out_ref[h, tok : tok + half, 0:HS] = v_ref[0:half, cols]
        out_ref[h, tok : tok + half, HS : 2 * HS] = v_ref[half:tok, cols]


def unpack_qkv_kernel(in_ref, q_ref, k_ref, v_ref):
    tok = q_ref.shape[0]
    half = tok // 2
    for h in range(q_ref.shape[1] // HS):
        cols = slice(h * HS, (h + 1) * HS)
        q_ref[:, cols] = in_ref[h, 0:tok, 0:HS]
        k_ref[:, cols] = in_ref[h, 0:tok, HS : 2 * HS]
        v_ref[0:half, cols] = in_ref[h, tok : tok + half, 0:HS]
        v_ref[half:tok, cols] = in_ref[h, tok : tok + half, HS : 2 * HS]


def grad_attention_kernel(cot_ref, w_ref, out_ref):
    tok = cot_ref.shape[0]
    half = tok // 2
    step = 4 * HS
    for c in range(w_ref.shape[0] // step):
        part = dg(cot_ref[...], w_ref[c * step : (c + 1) * step, :], 1, 1).astype(bf)
        for i in range(4):
            cols = slice(i * HS, (i + 1) * HS)
            out_ref[4 * c + i, :, 0:HS] = part[0:half, cols]
            out_ref[4 * c + i, :, HS : 2 * HS] = part[half:tok, cols]


def output_kernel(o_ref, w_ref, cot_ref, out_ref, gw_ref, att):
    tok = out_ref.shape[0]
    half = tok // 2
    for h in range(o_ref.shape[0]):
        cols = slice(h * HS, (h + 1) * HS)
        att[0:half, cols] = o_ref[h, :, 0:HS]
        att[half:tok, cols] = o_ref[h, :, HS : 2 * HS]
    width = w_ref.shape[1]
    for c in range(width // 512):
        cols = slice(c * 512, (c + 1) * 512)
        out_ref[:, cols] = dg(att[...], w_ref[:, cols], 1, 0).astype(bf)
    for c in range(att.shape[1] // 256):
        rows = slice(c * 256, (c + 1) * 256)
        gw_ref[rows, :] = dg(att[:, rows], cot_ref[...], 0, 0).astype(bf)


def unpack_heads(a_ref, qp, kp, vp):
    tok = 2 * a_ref.shape[1] // 3
    half = tok // 2
    length = a_ref.shape[0] * tok
    scale = jnp.asarray(HS**-0.5, bf)

    def one(t, c):
        first = pl.multiple_of(t * tok, tok)
        qp[pl.ds(first, tok), :] = a_ref[t, 0:tok, 0:HS] * scale
        kp[pl.ds(first, tok), :] = a_ref[t, 0:tok, HS : 2 * HS]
        vp[pl.ds(first, half), :] = a_ref[t, tok : tok + half, 0:HS]
        vp[pl.ds(first + half, half), :] = a_ref[t, tok : tok + half, HS : 2 * HS]
        return c

    lax.fori_loop(0, a_ref.shape[0], one, 0)
    kp[length : length + TAIL, :] = jnp.zeros((TAIL, HS), bf)
    vp[length : length + TAIL, :] = jnp.zeros((TAIL, HS), bf)


def fwd_kernel(a_ref, end_ref, o_ref, lse_ref, qp, kp, vp, acc, ml):
    unpack_heads(a_ref, qp, kp, vp)
    tok = 2 * a_ref.shape[1] // 3
    half = tok // 2
    length = a_ref.shape[0] * tok

    def tile(qh, h, k0, n, end):
        s = dg(kp[pl.ds(k0, n), :], qh, 1, 1)
        if end is not None:
            pos = lax.broadcasted_iota(jnp.int32, (n, QH), 0) + k0
            s = jnp.where(pos < end, s, NEG)
        m = ml[2 * h : 2 * h + 1, :]
        mn = jnp.maximum(m, jnp.max(s, axis=0, keepdims=True))
        p = jnp.exp(s - mn)
        al = jnp.exp(m - mn)
        ml[2 * h : 2 * h + 1, :] = mn
        ml[2 * h + 1 : 2 * h + 2, :] = ml[2 * h + 1 : 2 * h + 2, :] * al + jnp.sum(
            p, axis=0, keepdims=True
        )
        acc[h] = acc[h] * al + dg(vp[pl.ds(k0, n), :], p.astype(bf), 0, 0)

    def qblock(b, c):
        qs = pl.multiple_of(b * QB, QB)
        qh = [qp[pl.ds(qs + h * QH, QH), :] for h in range(2)]
        for h in range(2):
            ml[2 * h : 2 * h + 1, :] = jnp.full((1, QH), NEG, f32)
            ml[2 * h + 1 : 2 * h + 2, :] = jnp.zeros((1, QH), f32)
            acc[h] = jnp.zeros((HS, QH), f32)

        def kb(j, c):
            for h in range(2):
                tile(qh[h], h, pl.multiple_of(j * KT, KT), KT, None)
            return c

        lax.fori_loop(0, b, kb, 0)
        for h in range(2):
            tile(qh[h], h, qs, (h + 1) * QH + TAIL, end_ref[0:1, pl.ds(qs + h * QH, QH)])
        for h in range(2):
            total = ml[2 * h + 1 : 2 * h + 2, :]
            o = (acc[h] / total).T.astype(bf)
            for i in range(QH // tok):
                t = (QB // tok) * b + (QH // tok) * h + i
                o_ref[t, :, 0:HS] = o[i * tok : i * tok + half, :]
                o_ref[t, :, HS : 2 * HS] = o[i * tok + half : (i + 1) * tok, :]
            lse_ref[0:1, pl.ds(qs + h * QH, QH)] = ml[2 * h : 2 * h + 1, :] + jnp.log(total)
        return c

    lax.fori_loop(0, length // QB, qblock, 0)


def bwd_kernel(a_ref, do_ref, o_ref, end_ref, lse_ref, g_ref, qp, kp, vp, dqa, dka, dva):
    unpack_heads(a_ref, qp, kp, vp)
    tok = 2 * a_ref.shape[1] // 3
    half = tok // 2
    length = a_ref.shape[0] * tok
    dka[...] = jnp.zeros_like(dka)
    dva[...] = jnp.zeros_like(dva)

    def tile(qh, do, lse, dl, h, k0, n, end):
        r = pl.ds(k0, n)
        kk = kp[r, :]
        p = jnp.exp(dg(kk, qh, 1, 1) - lse)
        if end is not None:
            pos = lax.broadcasted_iota(jnp.int32, (n, QH), 0) + k0
            p = jnp.where(pos < end, p, 0.0)
        dp = dg(vp[r, :], do, 1, 1)
        dva[r, :] = dva[r, :] + dg(p.astype(bf), do, 1, 0)
        ds = (p * (dp - dl)).astype(bf)
        dka[r, :] = dka[r, :] + dg(ds, qh, 1, 0)
        dqa[h] = dqa[h] + dg(kk, ds, 0, 0)

    def halves(ref, t0):
        parts = []
        for i in range(QH // tok):
            parts.append(ref[t0 + i, :, 0:HS])
            parts.append(ref[t0 + i, :, HS : 2 * HS])
        return jnp.concatenate(parts, axis=0)

    def qblock(b, c):
        qs = pl.multiple_of(b * QB, QB)
        qh, do, lse, dl = [], [], [], []
        for h in range(2):
            r = pl.ds(qs + h * QH, QH)
            t0 = (QB // tok) * b + (QH // tok) * h
            qh.append(qp[r, :])
            do.append(halves(do_ref, t0))
            prod = do[h].astype(f32) * halves(o_ref, t0).astype(f32)
            dl.append(jnp.sum(prod.T, axis=0, keepdims=True))
            lse.append(lse_ref[0:1, r])
            dqa[h] = jnp.zeros((HS, QH), f32)

        def kb(j, c):
            for h in range(2):
                tile(qh[h], do[h], lse[h], dl[h], h, pl.multiple_of(j * KT, KT), KT, None)
            return c

        lax.fori_loop(0, b, kb, 0)
        for h in range(2):
            end = end_ref[0:1, pl.ds(qs + h * QH, QH)]
            tile(qh[h], do[h], lse[h], dl[h], h, qs, (h + 1) * QH + TAIL, end)
        for h in range(2):
            dq = (dqa[h] * (HS**-0.5)).T.astype(bf)
            for i in range(QH // tok):
                t = (QB // tok) * b + (QH // tok) * h + i
                g_ref[t, 0:tok, 0:HS] = dq[i * tok : (i + 1) * tok, :]
        return c

    lax.fori_loop(0, length // QB, qblock, 0)

    def finish(t, c):
        first = pl.multiple_of(t * tok, tok)
        g_ref[t, 0:tok, HS : 2 * HS] = dka[pl.ds(first, tok), :].astype(bf)
        g_ref[t, tok : tok + half, 0:HS] = dva[pl.ds(first, half), :].astype(bf)
        g_ref[t, tok : tok + half, HS : 2 * HS] = dva[pl.ds(first + half, half), :].astype(bf)
        return c

    lax.fori_loop(0, a_ref.shape[0], finish, 0)


def call(kernel, name, outs, args, scratch=(), flops=0, nbytes=0):
    return pl.pallas_call(
        kernel,
        out_shape=outs,
        in_specs=[VM] * len(args),
        out_specs=jax.tree.map(lambda _: VM, outs),
        scratch_shapes=list(scratch),
        compiler_params=pltpu.CompilerParams(vmem_limit_bytes=48 << 20),
        cost_estimate=pl.CostEstimate(flops=flops, bytes_accessed=nbytes, transcendentals=0),
        name=name,
    )(*args)


def exchange(array, axis):
    return lax.all_to_all(array, axis, split_axis=0, concat_axis=0, tiled=True)


def on_device(queries, keys, values, frames, out_weight, cotangent):
    tok, width = queries.shape[1], queries.shape[2]
    group = lax.axis_size("seq")
    length = tok * group
    sds = jax.ShapeDtypeStruct
    half = tok // 2

    packed = call(
        pack_qkv_kernel,
        "pack_qkv",
        sds((group, tok + half, 2 * HS), bf),
        (queries[0], keys[0], values[0]),
        nbytes=6 * tok * width,
    )
    heads = exchange(packed, "seq")
    weight = lax.all_gather(out_weight, "seq", axis=0, tiled=True)
    frame_all = lax.all_gather(frames[0], "seq", axis=0, tiled=True)
    end = lax.broadcasted_iota(jnp.int32, (1, length), 1) + 1
    padded = jnp.concatenate([frame_all, jnp.full((TAIL,), -1, jnp.int32)])
    for shift in range(1, TAIL):
        end = end + (padded[shift : shift + length] == frame_all).astype(jnp.int32)[None]

    cot = cotangent[0]
    grad_packed = call(
        grad_attention_kernel,
        "grad_attention",
        sds((group, half, 2 * HS), bf),
        (cot, weight),
        flops=2 * tok * width * width,
        nbytes=2 * width * width,
    )
    grad_heads = exchange(grad_packed, "seq")
    headbuf = pltpu.VMEM((length + TAIL, HS), bf)
    sumbuf = pltpu.VMEM((length + TAIL, HS), f32)
    o_packed, lse = call(
        fwd_kernel,
        "attention_forward",
        (sds((group, half, 2 * HS), bf), sds((1, length), f32)),
        (heads, end),
        (headbuf, headbuf, headbuf, pltpu.VMEM((2, HS, QH), f32), pltpu.VMEM((8, QH), f32)),
        flops=8 * length * length * HS // 2,
        nbytes=8 * length * HS,
    )
    o_tokens = exchange(o_packed, "seq")
    output, partial = call(
        output_kernel,
        "output_projection",
        (sds((tok, width), bf), sds((width, width), bf)),
        (o_tokens, weight, cot),
        (pltpu.VMEM((tok, width), bf),),
        flops=4 * tok * width * width,
        nbytes=4 * width * width,
    )
    grad_part = lax.psum_scatter(partial, "seq", scatter_dimension=0, tiled=True)
    grads = call(
        bwd_kernel,
        "attention_backward",
        sds((group, tok + half, 2 * HS), bf),
        (heads, grad_heads, o_packed, end, lse),
        (headbuf, headbuf, headbuf, pltpu.VMEM((2, HS, QH), f32), sumbuf, sumbuf),
        flops=20 * length * length * HS // 2,
        nbytes=16 * length * HS,
    )
    copies = jnp.broadcast_to(grad_part, (lax.axis_size("dp"), *grad_part.shape))
    grad_weight = exchange(copies, "dp").astype(f32).sum(axis=0)
    dq, dk, dv = call(
        unpack_qkv_kernel,
        "unpack_grads",
        (sds((tok, width), bf),) * 3,
        (exchange(grads, "seq"),),
        nbytes=6 * tok * width,
    )
    return output[None], dq[None], dk[None], dv[None], grad_weight


def solution(mesh):
    tokens = P("dp", "seq", None)
    return jax.shard_map(
        on_device,
        mesh=mesh,
        in_specs=(tokens, tokens, tokens, P("dp", "seq"), P("seq", None), tokens),
        out_specs=(tokens, tokens, tokens, tokens, P("seq", None)),
        check_vma=False,
    )
```

```python
import jax
import jax.numpy as jnp
from jax import lax
from jax.experimental import pallas as pl
from jax.experimental.pallas import tpu as pltpu
from jax.sharding import PartitionSpec as P

HS = 64
QB = 512
QH = 256
KT = 512
TAIL = 16
NEG = -1e30
f32, bf = jnp.float32, jnp.bfloat16
VM = pl.BlockSpec(memory_space=pltpu.VMEM)


def dg(a, b, ca, cb):
    return lax.dot_general(a, b, (((ca,), (cb,)), ((), ())), preferred_element_type=f32)


def pack_qkv_kernel(q_ref, k_ref, v_ref, frame_ref, cot_ref, out_ref, cols_ref):
    tok = q_ref.shape[0]
    half = tok // 2
    frame = frame_ref[...]
    row = lax.broadcasted_iota(jnp.int32, (TAIL, tok), 0)
    digits = jnp.where(row == 0, frame >> 4, jnp.where(row == 1, frame & 15, 0))
    digits = digits.astype(f32).astype(bf)
    part = cols_ref.shape[2]
    for d in range(cols_ref.shape[0]):
        cols_ref[d] = cot_ref[:, d * part : (d + 1) * part]
    for h in range(q_ref.shape[1] // HS):
        cols = slice(h * HS, (h + 1) * HS)
        out_ref[h, 0:tok, 0:HS] = q_ref[:, cols]
        out_ref[h, 0:tok, HS : 2 * HS] = k_ref[:, cols]
        out_ref[h, tok : tok + half, 0:HS] = v_ref[0:half, cols]
        out_ref[h, tok : tok + half, HS : 2 * HS] = v_ref[half:tok, cols]
        out_ref[h, tok + half : tok + half + TAIL, :] = digits


def unpack_qkv_kernel(in_ref, q_ref, k_ref, v_ref):
    tok = q_ref.shape[0]
    half = tok // 2
    for h in range(q_ref.shape[1] // HS):
        cols = slice(h * HS, (h + 1) * HS)
        q_ref[:, cols] = in_ref[h, 0:tok, 0:HS]
        k_ref[:, cols] = in_ref[h, 0:tok, HS : 2 * HS]
        v_ref[0:half, cols] = in_ref[h, tok : tok + half, 0:HS]
        v_ref[half:tok, cols] = in_ref[h, tok : tok + half, HS : 2 * HS]


def grad_attention_kernel(cot_ref, w_ref, out_ref):
    tok = cot_ref.shape[0]
    half = tok // 2
    step = 4 * HS
    for c in range(w_ref.shape[0] // step):
        part = dg(cot_ref[...], w_ref[c * step : (c + 1) * step, :], 1, 1).astype(bf)
        for i in range(4):
            cols = slice(i * HS, (i + 1) * HS)
            out_ref[4 * c + i, :, 0:HS] = part[0:half, cols]
            out_ref[4 * c + i, :, HS : 2 * HS] = part[half:tok, cols]


def output_kernel(o_ref, w_ref, out_ref, att):
    tok = out_ref.shape[0]
    half = tok // 2
    for h in range(o_ref.shape[0]):
        cols = slice(h * HS, (h + 1) * HS)
        att[0:half, cols] = o_ref[h, :, 0:HS]
        att[half:tok, cols] = o_ref[h, :, HS : 2 * HS]
    width = w_ref.shape[1]
    for c in range(width // 512):
        cols = slice(c * 512, (c + 1) * 512)
        out_ref[:, cols] = dg(att[...], w_ref[:, cols], 1, 0).astype(bf)


def weight_kernel(att_ref, cot_ref, gw_ref):
    for c in range(att_ref.shape[1] // 256):
        rows = slice(c * 256, (c + 1) * 256)
        gw_ref[rows, :] = dg(att_ref[:, rows], cot_ref[...], 0, 0).astype(bf)


def unpack_heads(a_ref, qp, kp, vp):
    tok = a_ref.shape[2]
    half = tok // 2
    length = a_ref.shape[0] * tok
    scale = jnp.asarray(HS**-0.5, bf)

    def one(t, c):
        first = pl.multiple_of(t * tok, tok)
        qp[pl.ds(first, tok), :] = a_ref[t, 0:tok, 0:HS] * scale
        kp[pl.ds(first, tok), :] = a_ref[t, 0:tok, HS : 2 * HS]
        vp[pl.ds(first, half), :] = a_ref[t, tok : tok + half, 0:HS]
        vp[pl.ds(first + half, half), :] = a_ref[t, tok : tok + half, HS : 2 * HS]
        return c

    lax.fori_loop(0, a_ref.shape[0], one, 0)
    kp[length : length + TAIL, :] = jnp.zeros((TAIL, HS), bf)
    vp[length : length + TAIL, :] = jnp.zeros((TAIL, HS), bf)


def row_ends(a_ref, end_ref, fr):
    tok = a_ref.shape[2]
    half = tok // 2
    blocks = a_ref.shape[0]

    def load(t, c):
        digits = a_ref[t, tok + half : tok + half + TAIL, :].astype(f32)
        fr[0:1, pl.ds(pl.multiple_of(t * tok, tok), tok)] = digits[0:1, :] * 16.0 + digits[1:2, :]
        return c

    lax.fori_loop(0, blocks, load, 0)
    fr[0:1, blocks * tok : (blocks + 1) * tok] = jnp.full((1, tok), -1.0, f32)

    def count(t, c):
        first = pl.multiple_of(t * tok, tok)
        wide = fr[0:1, pl.ds(first, 2 * tok)]
        own = wide[:, 0:tok]
        end = lax.broadcasted_iota(jnp.int32, (1, tok), 1) + (first + 1)
        for shift in range(1, TAIL):
            end = end + (wide[:, shift : shift + tok] == own).astype(jnp.int32)
        end_ref[0:1, pl.ds(first, tok)] = end
        return c

    lax.fori_loop(0, blocks, count, 0)


def fwd_kernel(a_ref, o_ref, lse_ref, end_ref, qp, kp, vp, acc, ml, fr):
    unpack_heads(a_ref, qp, kp, vp)
    row_ends(a_ref, end_ref, fr)
    tok = a_ref.shape[2]
    half = tok // 2
    length = a_ref.shape[0] * tok

    def tile(qh, h, k0, n, end):
        s = dg(kp[pl.ds(k0, n), :], qh, 1, 1)
        if end is not None:
            pos = lax.broadcasted_iota(jnp.int32, (n, QH), 0) + k0
            s = jnp.where(pos < end, s, NEG)
        m = ml[2 * h : 2 * h + 1, :]
        mn = jnp.maximum(m, jnp.max(s, axis=0, keepdims=True))
        p = jnp.exp(s - mn)
        al = jnp.exp(m - mn)
        ml[2 * h : 2 * h + 1, :] = mn
        ml[2 * h + 1 : 2 * h + 2, :] = ml[2 * h + 1 : 2 * h + 2, :] * al + jnp.sum(
            p, axis=0, keepdims=True
        )
        acc[h] = acc[h] * al + dg(vp[pl.ds(k0, n), :], p.astype(bf), 0, 0)

    def qblock(b, c):
        qs = pl.multiple_of(b * QB, QB)
        qh = [qp[pl.ds(qs + h * QH, QH), :] for h in range(2)]
        for h in range(2):
            ml[2 * h : 2 * h + 1, :] = jnp.full((1, QH), NEG, f32)
            ml[2 * h + 1 : 2 * h + 2, :] = jnp.zeros((1, QH), f32)
            acc[h] = jnp.zeros((HS, QH), f32)

        def kb(j, c):
            for h in range(2):
                tile(qh[h], h, pl.multiple_of(j * KT, KT), KT, None)
            return c

        lax.fori_loop(0, b, kb, 0)
        for h in range(2):
            tile(qh[h], h, qs, (h + 1) * QH + TAIL, end_ref[0:1, pl.ds(qs + h * QH, QH)])
        for h in range(2):
            total = ml[2 * h + 1 : 2 * h + 2, :]
            o = (acc[h] / total).T.astype(bf)
            for i in range(QH // tok):
                t = (QB // tok) * b + (QH // tok) * h + i
                o_ref[t, :, 0:HS] = o[i * tok : i * tok + half, :]
                o_ref[t, :, HS : 2 * HS] = o[i * tok + half : (i + 1) * tok, :]
            lse_ref[0:1, pl.ds(qs + h * QH, QH)] = ml[2 * h : 2 * h + 1, :] + jnp.log(total)
        return c

    lax.fori_loop(0, length // QB, qblock, 0)


def bwd_kernel(a_ref, do_ref, o_ref, end_ref, lse_ref, g_ref, qp, kp, vp, dqa, dka, dva):
    unpack_heads(a_ref, qp, kp, vp)
    tok = a_ref.shape[2]
    half = tok // 2
    length = a_ref.shape[0] * tok
    dka[...] = jnp.zeros_like(dka)
    dva[...] = jnp.zeros_like(dva)

    def tile(qh, do, lse, dl, h, k0, n, end):
        r = pl.ds(k0, n)
        kk = kp[r, :]
        p = jnp.exp(dg(kk, qh, 1, 1) - lse)
        if end is not None:
            pos = lax.broadcasted_iota(jnp.int32, (n, QH), 0) + k0
            p = jnp.where(pos < end, p, 0.0)
        dp = dg(vp[r, :], do, 1, 1)
        dva[r, :] = dva[r, :] + dg(p.astype(bf), do, 1, 0)
        ds = (p * (dp - dl)).astype(bf)
        dka[r, :] = dka[r, :] + dg(ds, qh, 1, 0)
        dqa[h] = dqa[h] + dg(kk, ds, 0, 0)

    def halves(ref, t0):
        parts = []
        for i in range(QH // tok):
            parts.append(ref[t0 + i, :, 0:HS])
            parts.append(ref[t0 + i, :, HS : 2 * HS])
        return jnp.concatenate(parts, axis=0)

    def qblock(b, c):
        qs = pl.multiple_of(b * QB, QB)
        qh, do, lse, dl = [], [], [], []
        for h in range(2):
            r = pl.ds(qs + h * QH, QH)
            t0 = (QB // tok) * b + (QH // tok) * h
            qh.append(qp[r, :])
            do.append(halves(do_ref, t0))
            prod = do[h].astype(f32) * halves(o_ref, t0).astype(f32)
            dl.append(jnp.sum(prod.T, axis=0, keepdims=True))
            lse.append(lse_ref[0:1, r])
            dqa[h] = jnp.zeros((HS, QH), f32)

        def kb(j, c):
            for h in range(2):
                tile(qh[h], do[h], lse[h], dl[h], h, pl.multiple_of(j * KT, KT), KT, None)
            return c

        lax.fori_loop(0, b, kb, 0)
        for h in range(2):
            end = end_ref[0:1, pl.ds(qs + h * QH, QH)]
            tile(qh[h], do[h], lse[h], dl[h], h, qs, (h + 1) * QH + TAIL, end)
        for h in range(2):
            dq = (dqa[h] * (HS**-0.5)).T.astype(bf)
            for i in range(QH // tok):
                t = (QB // tok) * b + (QH // tok) * h + i
                g_ref[t, 0:tok, 0:HS] = dq[i * tok : (i + 1) * tok, :]
        return c

    lax.fori_loop(0, length // QB, qblock, 0)

    def finish(t, c):
        first = pl.multiple_of(t * tok, tok)
        g_ref[t, 0:tok, HS : 2 * HS] = dka[pl.ds(first, tok), :].astype(bf)
        g_ref[t, tok : tok + half, 0:HS] = dva[pl.ds(first, half), :].astype(bf)
        g_ref[t, tok : tok + half, HS : 2 * HS] = dva[pl.ds(first + half, half), :].astype(bf)
        return c

    lax.fori_loop(0, a_ref.shape[0], finish, 0)


def call(kernel, name, outs, args, scratch=(), flops=0, nbytes=0):
    return pl.pallas_call(
        kernel,
        out_shape=outs,
        in_specs=[VM] * len(args),
        out_specs=jax.tree.map(lambda _: VM, outs),
        scratch_shapes=list(scratch),
        compiler_params=pltpu.CompilerParams(vmem_limit_bytes=48 << 20),
        cost_estimate=pl.CostEstimate(flops=flops, bytes_accessed=nbytes, transcendentals=0),
        name=name,
    )(*args)


def exchange(array, axis):
    return lax.all_to_all(array, axis, split_axis=0, concat_axis=0, tiled=True)


def on_device(queries, keys, values, frames, out_weight, cotangent):
    tok, width = queries.shape[1], queries.shape[2]
    group = lax.axis_size("seq")
    length = tok * group
    sds = jax.ShapeDtypeStruct
    half = tok // 2

    clips = lax.axis_size("dp")
    cot = cotangent[0]
    packed, cot_cols = call(
        pack_qkv_kernel,
        "pack_qkv",
        (sds((group, tok + half + TAIL, 2 * HS), bf), sds((clips, tok, width // clips), bf)),
        (queries[0], keys[0], values[0], frames, cot),
        nbytes=6 * tok * width,
    )
    heads = exchange(packed, "seq")
    weight = lax.all_gather(out_weight, "seq", axis=0, tiled=True)
    cot_group = exchange(cot_cols, "dp").reshape(clips * tok, width // clips)
    grad_packed = call(
        grad_attention_kernel,
        "grad_attention",
        sds((group, half, 2 * HS), bf),
        (cot, weight),
        flops=2 * tok * width * width,
        nbytes=2 * width * width,
    )
    grad_heads = exchange(grad_packed, "seq")
    headbuf = pltpu.VMEM((length + TAIL, HS), bf)
    sumbuf = pltpu.VMEM((length + TAIL, HS), f32)
    o_packed, lse, end = call(
        fwd_kernel,
        "attention_forward",
        (
            sds((group, half, 2 * HS), bf),
            sds((1, length), f32),
            sds((1, length), jnp.int32),
        ),
        (heads,),
        (
            headbuf,
            headbuf,
            headbuf,
            pltpu.VMEM((2, HS, QH), f32),
            pltpu.VMEM((8, QH), f32),
            pltpu.VMEM((1, length + tok), f32),
        ),
        flops=8 * length * length * HS // 2,
        nbytes=8 * length * HS,
    )
    o_tokens = exchange(o_packed, "seq")
    output, att = call(
        output_kernel,
        "output_projection",
        (sds((tok, width), bf), sds((tok, width), bf)),
        (o_tokens, weight),
        flops=2 * tok * width * width,
        nbytes=2 * width * width,
    )
    att_group = lax.all_gather(att, "dp", axis=0, tiled=True)
    partial = call(
        weight_kernel,
        "weight_partial",
        sds((width, width // clips), bf),
        (att_group, cot_group),
        flops=2 * tok * width * width,
        nbytes=2 * width * tok * clips,
    )
    grad_part = lax.psum_scatter(partial, "seq", scatter_dimension=0, tiled=True)
    grad_weight = lax.all_gather(grad_part, "dp", axis=1, tiled=True).astype(f32)
    grads = call(
        bwd_kernel,
        "attention_backward",
        sds((group, tok + half, 2 * HS), bf),
        (heads, grad_heads, o_packed, end, lse),
        (headbuf, headbuf, headbuf, pltpu.VMEM((2, HS, QH), f32), sumbuf, sumbuf),
        flops=20 * length * length * HS // 2,
        nbytes=16 * length * HS,
    )
    dq, dk, dv = call(
        unpack_qkv_kernel,
        "unpack_grads",
        (sds((tok, width), bf),) * 3,
        (exchange(grads, "seq"),),
        nbytes=6 * tok * width,
    )
    return output[None], dq[None], dk[None], dv[None], grad_weight


def solution(mesh):
    tokens = P("dp", "seq", None)
    return jax.shard_map(
        on_device,
        mesh=mesh,
        in_specs=(tokens, tokens, tokens, P("dp", "seq"), P("seq", None), tokens),
        out_specs=(tokens, tokens, tokens, tokens, P("seq", None)),
        check_vma=False,
    )
```

```python
import jax
import jax.numpy as jnp
from jax import lax
from jax.experimental import pallas as pl
from jax.experimental.pallas import tpu as pltpu
from jax.sharding import PartitionSpec as P

HS = 64
QB = 512
QH = 256
TAIL = 16
NEG = -1e30
NX, NY, NZH, NZL = 4, 4, 4, 2
f32, bf = jnp.float32, jnp.bfloat16
VM = pl.BlockSpec(memory_space=pltpu.VMEM)
MESH = pl.DeviceIdType.MESH


def dg(a, b, ca, cb):
    return lax.dot_general(a, b, (((ca,), (cb,)), ((), ())), preferred_element_type=f32)


def place():
    d, s = lax.axis_index("dp"), lax.axis_index("seq")
    return d, s


def remote(src, dst, send, recv, device):
    return pltpu.make_async_remote_copy(
        src_ref=src, dst_ref=dst, send_sem=send, recv_sem=recv, device_id=device, device_id_type=MESH
    )


def others(count, me, body):
    def one(i, c):
        body((me + i) % count)
        return c

    lax.fori_loop(1, count, one, 0)


def forward_kernel(
    q_ref, k_ref, v_ref, frame_ref, cot_ref,
    qp, kp, vp, end_ref, lse_ref, osend, orecv, cotg,
    send, recv, fr, acc, ml,
    qkv_s, qkv_r, o_s, o_r, c_s, c_r,
):
    d, me = place()
    y, zl = d // NZL, d % NZL
    tok = q_ref.shape[0]
    half = tok // 2
    blocks = send.shape[0]
    length = blocks * tok
    quarter = cotg.shape[1]

    barrier = pltpu.get_barrier_semaphore()

    def greet(t):
        pl.semaphore_signal(barrier, inc=1, device_id=(d, t), device_id_type=MESH)

    def greet_y(t):
        pl.semaphore_signal(barrier, inc=1, device_id=(t * NZL + zl, me), device_id_type=MESH)

    others(blocks, me, greet)
    others(NY, y, greet_y)

    frame = frame_ref[...]
    row = lax.broadcasted_iota(jnp.int32, (TAIL, tok), 0)
    digits = jnp.where(row == 0, frame >> 4, jnp.where(row == 1, frame & 15, 0))
    digits = digits.astype(f32).astype(bf)
    for h in range(blocks):
        cols = slice(h * HS, (h + 1) * HS)
        send[h, 0:tok, 0:HS] = q_ref[:, cols]
        send[h, 0:tok, HS : 2 * HS] = k_ref[:, cols]
        send[h, tok : tok + half, 0:HS] = v_ref[0:half, cols]
        send[h, tok : tok + half, HS : 2 * HS] = v_ref[half:tok, cols]
        send[h, tok + half : tok + half + TAIL, :] = digits
    pl.semaphore_wait(barrier, blocks - 1 + NY - 1)

    def qkv(t, src):
        return remote(send.at[t], recv.at[src], qkv_s.at[t], qkv_r.at[src], (d, t))

    def cot_copy(t, src):
        cols = pl.ds(pl.multiple_of(t * quarter, quarter), quarter)
        rows = pl.ds(pl.multiple_of(src * tok, tok), tok)
        return remote(
            cot_ref.at[:, cols], cotg.at[rows, :], c_s.at[t], c_r.at[src], (t * NZL + zl, me)
        )

    others(blocks, me, lambda t: qkv(t, me).start())
    others(NY, y, lambda t: cot_copy(t, y).start())
    recv[me] = send[me]
    cotg[pl.ds(pl.multiple_of(y * tok, tok), tok), :] = cot_ref[
        :, pl.ds(pl.multiple_of(y * quarter, quarter), quarter)
    ]
    others(blocks, me, lambda t: qkv(t, t).wait_recv())

    scale = jnp.asarray(HS**-0.5, bf)

    def unpack(t, c):
        first = pl.multiple_of(t * tok, tok)
        qp[pl.ds(first, tok), :] = recv[t, 0:tok, 0:HS] * scale
        kp[pl.ds(first, tok), :] = recv[t, 0:tok, HS : 2 * HS]
        vp[pl.ds(first, half), :] = recv[t, tok : tok + half, 0:HS]
        vp[pl.ds(first + half, half), :] = recv[t, tok : tok + half, HS : 2 * HS]
        dig = recv[t, tok + half : tok + half + TAIL, :].astype(f32)
        fr[0:1, pl.ds(first, tok)] = dig[0:1, :] * 16.0 + dig[1:2, :]
        return c

    lax.fori_loop(0, blocks, unpack, 0)
    kp[length : length + TAIL, :] = jnp.zeros((TAIL, HS), bf)
    vp[length : length + TAIL, :] = jnp.zeros((TAIL, HS), bf)
    fr[0:1, length : length + tok] = jnp.full((1, tok), -1.0, f32)

    def count(t, c):
        first = pl.multiple_of(t * tok, tok)
        wide = fr[0:1, pl.ds(first, 2 * tok)]
        own = wide[:, 0:tok]
        end = lax.broadcasted_iota(jnp.int32, (1, tok), 1) + (first + 1)
        for shift in range(1, TAIL):
            end = end + (wide[:, shift : shift + tok] == own).astype(jnp.int32)
        end_ref[0:1, pl.ds(first, tok)] = end
        return c

    lax.fori_loop(0, blocks, count, 0)

    def o_copy(t, src):
        return remote(osend.at[t], orecv.at[src], o_s.at[t], o_r.at[src], (d, t))

    def tile(qh, h, k0, n, end):
        s = dg(kp[pl.ds(k0, n), :], qh, 1, 1)
        if end is not None:
            pos = lax.broadcasted_iota(jnp.int32, (n, QH), 0) + k0
            s = jnp.where(pos < end, s, NEG)
        m = ml[2 * h : 2 * h + 1, :]
        mn = jnp.maximum(m, jnp.max(s, axis=0, keepdims=True))
        p = jnp.exp(s - mn)
        al = jnp.exp(m - mn)
        ml[2 * h : 2 * h + 1, :] = mn
        ml[2 * h + 1 : 2 * h + 2, :] = ml[2 * h + 1 : 2 * h + 2, :] * al + jnp.sum(
            p, axis=0, keepdims=True
        )
        acc[h] = acc[h] * al + dg(vp[pl.ds(k0, n), :], p.astype(bf), 0, 0)

    def qblock(i, c):
        b = (i + me) % (length // QB)
        qs = pl.multiple_of(b * QB, QB)
        qh = [qp[pl.ds(qs + h * QH, QH), :] for h in range(2)]
        for h in range(2):
            ml[2 * h : 2 * h + 1, :] = jnp.full((1, QH), NEG, f32)
            ml[2 * h + 1 : 2 * h + 2, :] = jnp.zeros((1, QH), f32)
            acc[h] = jnp.zeros((HS, QH), f32)

        def kb(j, c):
            for h in range(2):
                tile(qh[h], h, pl.multiple_of(j * QB, QB), QB, None)
            return c

        lax.fori_loop(0, b, kb, 0)
        for h in range(2):
            tile(qh[h], h, qs, (h + 1) * QH + TAIL, end_ref[0:1, pl.ds(qs + h * QH, QH)])
        for h in range(2):
            total = ml[2 * h + 1 : 2 * h + 2, :]
            o = (acc[h] / total).T.astype(bf)
            for n in range(QH // tok):
                t = (QB // tok) * b + (QH // tok) * h + n
                osend[t, :, 0:HS] = o[n * tok : n * tok + half, :]
                osend[t, :, HS : 2 * HS] = o[n * tok + half : (n + 1) * tok, :]

            lse_ref[0:1, pl.ds(qs + h * QH, QH)] = ml[2 * h : 2 * h + 1, :] + jnp.log(total)
        for n in range(QB // tok):
            t = (QB // tok) * b + n

            @pl.when(t != me)
            def _():
                o_copy(t, me).start()

            @pl.when(t == me)
            def _():
                orecv[t] = osend[t]

        return c

    lax.fori_loop(0, length // QB, qblock, 0)

    others(blocks, me, lambda t: o_copy(t, t).wait_recv())
    others(NY, y, lambda t: cot_copy(t, t).wait_recv())
    others(blocks, me, lambda t: o_copy(t, me).wait_send())
    others(blocks, me, lambda t: qkv(t, me).wait_send())
    others(NY, y, lambda t: cot_copy(t, y).wait_send())


def backward_kernel(
    qp, kp, vp, end_ref, lse_ref, own_o, tok_o, cotg, w_ref, cot_ref,
    out_ref, dq_ref, dk_ref, dv_ref, gw_ref,
    attg, dosend, dorecv, dop, dl, kvsend, kvrecv, dqsend, dqrecv, dqt, dka, dva,
    gwp, s1recv, s2send, s2recv, piece,
    do_s, do_r, kv_s, kv_r, dq_s, dq_r, a_s, a_r, g1_s, g1_r, g2_s, g2_r, g3_s, g3_r,
):
    d, me = place()
    y, zl = d // NZL, d % NZL
    x, zh, core = me // (2 * NZH), (me // 2) % NZH, me % 2
    tok = out_ref.shape[0]
    half = tok // 2
    blocks = dosend.shape[0]
    length = blocks * tok
    steps = length // QB
    xc, zz = x * 2 + core, zh * NZL + zl
    wide = cotg.shape[1]
    dps = NY * NZL

    barrier = pltpu.get_barrier_semaphore()

    def greet(dev):
        pl.semaphore_signal(barrier, inc=1, device_id=dev, device_id_type=MESH)

    others(blocks, me, lambda t: greet((d, t)))
    others(dps, d, lambda t: greet((t, me)))
    across = y * NZL + (1 - zl)
    others(NZH, zh, lambda t: greet((across, x * 2 * NZH + t * 2 + core)))

    def do_copy(t, src):
        return remote(dosend.at[t], dorecv.at[src], do_s.at[t], do_r.at[src], (d, t))

    def kv_copy(t, src):
        return remote(kvsend.at[t], kvrecv.at[src], kv_s.at[t], kv_r.at[src], (d, t))

    def dq_copy(t, src):
        return remote(dqsend.at[t], dqrecv.at[src], dq_s.at[t], dq_r.at[src], (d, t))

    def att_copy(t, src):
        mine = pl.ds(pl.multiple_of(y * tok, tok), tok)
        rows = pl.ds(pl.multiple_of(src * tok, tok), tok)
        return remote(attg.at[mine, :], attg.at[rows, :], a_s.at[t], a_r.at[src], (t * NZL + zl, me))

    def g1_copy(t, src):
        dev = (d, (t // 2) * 2 * NZH + zh * 2 + t % 2)
        return remote(gwp.at[t], s1recv.at[src], g1_s.at[t], g1_r.at[src], dev)

    def g2_copy(t, src):
        dev = (y * NZL + t % NZL, x * 2 * NZH + (t // NZL) * 2 + core)
        return remote(s2send.at[t], s2recv.at[src], g2_s.at[t], g2_r.at[src], dev)

    def g3_copy(t, src):
        rows = pl.ds(pl.multiple_of((src % NZL) * (HS // NZL), HS // NZL), HS // NZL)
        cols = pl.ds(pl.multiple_of((src // NZL) * wide, wide), wide)
        return remote(piece, gw_ref.at[rows, cols], g3_s.at[t], g3_r.at[src], (t, me))

    first = pl.ds(pl.multiple_of(y * tok, tok), tok)
    upper = pl.ds(pl.multiple_of(y * tok, tok), half)
    lower = pl.ds(pl.multiple_of(y * tok + half, half), half)
    for h in range(blocks):
        cols = slice(h * HS, (h + 1) * HS)
        attg[upper, cols] = tok_o[h, :, 0:HS]
        attg[lower, cols] = tok_o[h, :, HS : 2 * HS]
    pl.semaphore_wait(barrier, blocks - 1 + dps - 1 + NZH - 1)
    others(NY, y, lambda t: att_copy(t, y).start())

    def grad_heads(i, c):
        g = (i + me // 4) % (blocks // 4)
        rows = pl.ds(pl.multiple_of(g * 4 * HS, 4 * HS), 4 * HS)
        part = dg(cot_ref[...], w_ref[rows, :], 1, 1).astype(bf)
        for n in range(4):
            t = 4 * g + n
            cols = slice(n * HS, (n + 1) * HS)
            dosend[t, :, 0:HS] = part[0:half, cols]
            dosend[t, :, HS : 2 * HS] = part[half:tok, cols]
        for n in range(4):
            t = 4 * g + n

            @pl.when(t != me)
            def _():
                do_copy(t, me).start()

            @pl.when(t == me)
            def _():
                dorecv[t] = dosend[t]

        return c

    lax.fori_loop(0, blocks // 4, grad_heads, 0)

    def project(i, c):
        cols = pl.ds(pl.multiple_of(i * 512, 512), 512)
        out_ref[:, cols] = dg(attg[first, :], w_ref[:, cols], 1, 0).astype(bf)
        return c

    lax.fori_loop(0, out_ref.shape[1] // 512, project, 0)
    dqt[...] = jnp.zeros_like(dqt)
    others(blocks, me, lambda t: do_copy(t, t).wait_recv())

    def deltas(t, c):
        a = pl.multiple_of(t * tok, tok)
        up, lo = dorecv[t, :, 0:HS], dorecv[t, :, HS : 2 * HS]
        dop[pl.ds(a, half), :] = up
        dop[pl.ds(a + half, half), :] = lo
        prod = dorecv[t].astype(f32) * own_o[t].astype(f32)
        turned = prod.T
        both = [jnp.sum(turned[n * HS : (n + 1) * HS, :], axis=0, keepdims=True) for n in range(2)]
        dl[0:1, pl.ds(a, tok)] = jnp.concatenate(both, axis=1)
        return c

    lax.fori_loop(0, blocks, deltas, 0)

    def tile(k0, a, n, q0, width, masked):
        qr = pl.ds(q0, width)
        kr = pl.ds(k0 + a, n)
        kk, qh, do = kp[kr, :], qp[qr, :], dop[qr, :]
        p = jnp.exp(dg(kk, qh, 1, 1) - lse_ref[0:1, qr])
        if masked:
            pos = lax.broadcasted_iota(jnp.int32, (n, width), 0) + (k0 + a)
            p = jnp.where(pos < end_ref[0:1, qr], p, 0.0)
        dp = dg(vp[kr, :], do, 1, 1)
        dva[a : a + n, :] = dva[a : a + n, :] + dg(p.astype(bf), do, 1, 0)
        ds = (p * (dp - dl[0:1, qr])).astype(bf)
        dka[a : a + n, :] = dka[a : a + n, :] + dg(ds, qh, 1, 0)
        dqt[:, qr] = dqt[:, qr] + dg(kk, ds, 0, 0)

    def kblock(i, c):
        j = (i + me) % steps
        ks = pl.multiple_of(j * QB, QB)
        dka[...] = jnp.zeros_like(dka)
        dva[...] = jnp.zeros_like(dva)

        @pl.when(j > 0)
        def _():
            tile(ks, 0, TAIL, pl.multiple_of(ks - tok, tok), tok, True)

        tile(ks, 0, QH + TAIL, ks, QH, True)
        tile(ks, 0, QB, pl.multiple_of(ks + QH, QH), QH, True)

        def later(b, c):
            qs = pl.multiple_of(b * QB, QB)
            for h in range(2):
                tile(ks, 0, QB, pl.multiple_of(qs + h * QH, QH), QH, False)
            return c

        lax.fori_loop(j + 1, steps, later, 0)
        for n in range(QB // tok):
            t = (QB // tok) * j + n
            kvsend[t, :, 0:HS] = dka[n * tok : (n + 1) * tok, :].astype(bf)
            kvsend[t, :, HS : 2 * HS] = dva[n * tok : (n + 1) * tok, :].astype(bf)
        for n in range(QB // tok):
            t = (QB // tok) * j + n

            @pl.when(t != me)
            def _():
                kv_copy(t, me).start()

            @pl.when(t == me)
            def _():
                kvrecv[t] = kvsend[t]

        @pl.when(i == 2)
        def _():
            others(NY, y, lambda t: att_copy(t, t).wait_recv())
            for g in range(blocks // 4):
                part = dg(attg[:, g * 4 * HS : (g + 1) * 4 * HS], cotg[...], 0, 0).astype(bf)
                for n in range(4):
                    h = 4 * g + n
                    to = (h // (2 * NZH)) * 2 + h % 2
                    at = ((h // 2) % NZH) * HS
                    gwp[to, at : at + HS, :] = part[n * HS : (n + 1) * HS, :]
            others(2 * NX, xc, lambda t: g1_copy(t, xc).start())

        @pl.when(i == 5)
        def _():
            others(2 * NX, xc, lambda t: g1_copy(t, t).wait_recv())
            s1recv[xc] = gwp[xc]
            for n in range(NZH * NZL):
                rows = slice(n * (HS // NZL), (n + 1) * (HS // NZL))
                total = s1recv[0, rows, :].astype(f32)
                for m in range(1, 2 * NX):
                    total = total + s1recv[m, rows, :].astype(f32)
                s2send[n] = total.astype(bf)
            others(NZH * NZL, zz, lambda t: g2_copy(t, zz).start())

        return c

    lax.fori_loop(0, steps, kblock, 0)

    def queries_done(i, c):
        t = (i + me) % blocks
        a = pl.multiple_of(t * tok, tok)
        dq = (dqt[:, pl.ds(a, tok)] * (HS**-0.5)).T.astype(bf)
        dqsend[t, :, 0:HS] = dq[0:half, :]
        dqsend[t, :, HS : 2 * HS] = dq[half:tok, :]

        @pl.when(t != me)
        def _():
            dq_copy(t, me).start()

        @pl.when(t == me)
        def _():
            dqrecv[t] = dqsend[t]

        return c

    lax.fori_loop(0, blocks, queries_done, 0)

    others(NZH * NZL, zz, lambda t: g2_copy(t, t).wait_recv())
    s2recv[zz] = s2send[zz]
    total = s2recv[0].astype(f32)
    for m in range(1, NZH * NZL):
        total = total + s2recv[m].astype(f32)
    piece[...] = total
    others(dps, d, lambda t: g3_copy(t, d).start())
    gw_ref[
        pl.ds(pl.multiple_of(zl * (HS // NZL), HS // NZL), HS // NZL),
        pl.ds(pl.multiple_of(y * wide, wide), wide),
    ] = total

    others(blocks, me, lambda t: kv_copy(t, t).wait_recv())
    for h in range(blocks):
        cols = slice(h * HS, (h + 1) * HS)
        dk_ref[:, cols] = kvrecv[h, :, 0:HS]
        dv_ref[:, cols] = kvrecv[h, :, HS : 2 * HS]
    others(blocks, me, lambda t: dq_copy(t, t).wait_recv())
    for h in range(blocks):
        cols = slice(h * HS, (h + 1) * HS)
        dq_ref[0:half, cols] = dqrecv[h, :, 0:HS]
        dq_ref[half:tok, cols] = dqrecv[h, :, HS : 2 * HS]
    others(dps, d, lambda t: g3_copy(t, t).wait_recv())
    others(blocks, me, lambda t: do_copy(t, me).wait_send())
    others(blocks, me, lambda t: kv_copy(t, me).wait_send())
    others(blocks, me, lambda t: dq_copy(t, me).wait_send())
    others(NY, y, lambda t: att_copy(t, y).wait_send())
    others(2 * NX, xc, lambda t: g1_copy(t, xc).wait_send())
    others(NZH * NZL, zz, lambda t: g2_copy(t, zz).wait_send())
    others(dps, d, lambda t: g3_copy(t, d).wait_send())


def call(kernel, name, cid, outs, args, scratch, flops, nbytes):
    return pl.pallas_call(
        kernel,
        out_shape=outs,
        in_specs=[VM] * len(args),
        out_specs=jax.tree.map(lambda _: VM, outs),
        scratch_shapes=scratch,
        compiler_params=pltpu.CompilerParams(
            vmem_limit_bytes=56 << 20, collective_id=cid, has_side_effects=True
        ),
        cost_estimate=pl.CostEstimate(flops=flops, bytes_accessed=nbytes, transcendentals=0),
        name=name,
    )(*args)


def on_device(queries, keys, values, frames, out_weight, cotangent):
    tok, width = queries.shape[1], queries.shape[2]
    group = lax.axis_size("seq")
    length = tok * group
    half = tok // 2
    sds = jax.ShapeDtypeStruct
    vmem = pltpu.VMEM

    def sems(n):
        return [pltpu.SemaphoreType.DMA((n,))] * 2

    weight = lax.all_gather(out_weight, "seq", axis=0, tiled=True)
    cot = cotangent[0]
    packed = (group, half, 2 * HS)
    qp, kp, vp, end, lse, own_o, tok_o, cotg = call(
        forward_kernel,
        "attention_forward",
        0,
        (
            sds((length, HS), bf),
            sds((length + TAIL, HS), bf),
            sds((length + TAIL, HS), bf),
            sds((1, length), jnp.int32),
            sds((1, length), f32),
            sds(packed, bf),
            sds(packed, bf),
            sds((NY * tok, width // NY), bf),
        ),
        (queries[0], keys[0], values[0], frames, cot),
        [
            vmem((group, tok + half + TAIL, 2 * HS), bf),
            vmem((group, tok + half + TAIL, 2 * HS), bf),
            vmem((1, length + tok), f32),
            vmem((2, HS, QH), f32),
            vmem((8, QH), f32),
            *sems(group),
            *sems(group),
            *sems(NY),
        ],
        8 * length * length * HS,
        8 * length * HS,
    )
    output, dq, dk, dv, gw = call(
        backward_kernel,
        "attention_backward",
        1,
        (sds((tok, width), bf),) * 4 + (sds((HS, width), f32),),
        (qp, kp, vp, end, lse, own_o, tok_o, cotg, weight, cot),
        [
            vmem((NY * tok, width), bf),
            vmem(packed, bf),
            vmem(packed, bf),
            vmem((length, HS), bf),
            vmem((1, length), f32),
            vmem((group, tok, 2 * HS), bf),
            vmem((group, tok, 2 * HS), bf),
            vmem(packed, bf),
            vmem(packed, bf),
            vmem((HS, length), f32),
            vmem((QB, HS), f32),
            vmem((QB, HS), f32),
            vmem((2 * NX, NZH * HS, width // NY), bf),
            vmem((2 * NX, NZH * HS, width // NY), bf),
            vmem((NZH * NZL, HS // NZL, width // NY), bf),
            vmem((NZH * NZL, HS // NZL, width // NY), bf),
            vmem((HS // NZL, width // NY), f32),
            *sems(group),
            *sems(group),
            *sems(group),
            *sems(NY),
            *sems(2 * NX),
            *sems(NZH * NZL),
            *sems(NY * NZL),
        ],
        20 * length * length * HS,
        16 * length * HS,
    )
    return output[None], dq[None], dk[None], dv[None], gw


def solution(mesh):
    tokens = P("dp", "seq", None)
    return jax.shard_map(
        on_device,
        mesh=mesh,
        in_specs=(tokens, tokens, tokens, P("dp", "seq"), P("seq", None), tokens),
        out_specs=(tokens, tokens, tokens, tokens, P("seq", None)),
        check_vma=False,
    )
```

```python
import jax
import jax.numpy as jnp
from jax import lax
from jax.experimental import pallas as pl
from jax.experimental.pallas import tpu as pltpu
from jax.sharding import PartitionSpec as P

HS = 64
QB = 512
QH = 256
TAIL = 16
NEG = -1e30
NX, NY, NZH, NZL = 4, 4, 4, 2
f32, bf = jnp.float32, jnp.bfloat16
VM = pl.BlockSpec(memory_space=pltpu.VMEM)
MESH = pl.DeviceIdType.MESH


def dg(a, b, ca, cb):
    return lax.dot_general(a, b, (((ca,), (cb,)), ((), ())), preferred_element_type=f32)


def place():
    d, s = lax.axis_index("dp"), lax.axis_index("seq")
    return d, s


def remote(src, dst, send, recv, device):
    return pltpu.make_async_remote_copy(
        src_ref=src, dst_ref=dst, send_sem=send, recv_sem=recv, device_id=device, device_id_type=MESH
    )


def others(count, me, body):
    def one(i, c):
        body((me + i) % count)
        return c

    lax.fori_loop(1, count, one, 0)


def kernel(
    q_ref, k_ref, v_ref, frame_ref, cot_ref, w_ref,
    out_ref, dq_ref, dk_ref, dv_ref, gw_ref,
    send, recv, qp, kp, vp, fr, end_ref, lse_ref, acc, ml,
    wp, cotg, dysend, dyrecv, dosend, dot, ot, orecv, aysend, attp,
    kvsend, kvrecv, dqsend, dqrecv, dqt, dka, dva, dl,
    gwp, s1recv, s2send, s2recv, piece, psend, precv,
    qkv_s, qkv_r, do_s, do_r, o_s, o_r, kv_s, kv_r, dq_s, dq_r,
    c_s, c_r, dy_s, dy_r, ay_s, ay_r, p_s, p_r,
    w1_s, w1_r, w2_s, w2_r, w3_s, w3_r, g1_s, g1_r, g2_s, g2_r, g3_s, g3_r,
):
    d, me = place()
    y, zl = d // NZL, d % NZL
    x, zh, core = me // (2 * NZH), (me // 2) % NZH, me % 2
    xc, zz = x * 2 + core, zh * NZL + zl
    tok, width = q_ref.shape
    half = tok // 2
    blocks = send.shape[0]
    length = blocks * tok
    steps = length // QB
    per = HS // NY
    group = blocks // 2 * per
    dps = NY * NZL

    def seq_of(xx, zz_, cc):
        return xx * 2 * NZH + zz_ * 2 + cc

    def ydev(t):
        return (t * NZL + zl, me)

    def al(v, n):
        return pl.ds(pl.multiple_of(v * n, n), n)

    def row_of(h):
        return (h % 2) * group + (h // 2) * per

    barrier = pltpu.get_barrier_semaphore()

    def greet(dev):
        pl.semaphore_signal(barrier, inc=1, device_id=dev, device_id_type=MESH)

    others(blocks, me, lambda t: greet((d, t)))
    others(dps, d, lambda t: greet((t, me)))
    others(NZH, zh, lambda t: greet((y * NZL + (1 - zl), seq_of(x, t, core))))

    def qkv(t, src):
        return remote(send.at[t], recv.at[src], qkv_s.at[t], qkv_r.at[src], (d, t))

    def cot_copy(t, src):
        return remote(cot_ref, cotg.at[al(src, tok), :], c_s.at[t], c_r.at[src], ydev(t))

    def w1_copy(t, src):
        at = wp.at[core, pl.ds(pl.multiple_of((x * NZH + src) * per, per), per), :]
        return remote(w_ref.at[al(y, per), :], at, w1_s.at[t], w1_r.at[src], (d, seq_of(x, t, core)))

    def w2_copy(t, src):
        own = wp.at[core, al(x, NZH * per), :]
        at = wp.at[core, al(src, NZH * per), :]
        return remote(own, at, w2_s.at[t], w2_r.at[src], (d, seq_of(t, zh, core)))

    def w3_copy(c):
        return remote(wp.at[c], wp.at[c], w3_s.at[0], w3_r.at[0], (d, seq_of(x, zh, 1 - core)))

    def dy_copy(c, t, src):
        return remote(
            dysend.at[c, t], dyrecv.at[c, src], dy_s.at[c, t], dy_r.at[c, src], ydev(t)
        )

    def do_copy(t, src):
        return remote(dosend.at[t], dot.at[:, al(src, tok)], do_s.at[t], do_r.at[src], (d, t))

    def o_copy(t, src):
        return remote(ot.at[:, al(t, tok)], orecv.at[src], o_s.at[t], o_r.at[src], (d, t))

    def ay_copy(t, src):
        return remote(aysend.at[t], attp.at[:, al(src, tok)], ay_s.at[t], ay_r.at[src], ydev(t))

    def p_copy(t, src):
        return remote(psend.at[t], precv.at[src], p_s.at[t], p_r.at[src], ydev(t))

    def kv_copy(t, src):
        return remote(kvsend.at[t], kvrecv.at[src], kv_s.at[t], kv_r.at[src], (d, t))

    def dq_copy(t, src):
        return remote(dqsend.at[t], dqrecv.at[src], dq_s.at[t], dq_r.at[src], (d, t))

    def g1_copy(t, src):
        rows = pl.ds(pl.multiple_of((t % 2) * group + (t // 2) * NZH * per, NZH * per), NZH * per)
        dev = (d, seq_of(t // 2, zh, t % 2))
        return remote(gwp.at[rows, :], s1recv.at[src], g1_s.at[t], g1_r.at[src], dev)

    def g2_copy(t, src):
        dev = (y * NZL + t % NZL, seq_of(x, t // NZL, core))
        return remote(s2send.at[t], s2recv.at[src], g2_s.at[t], g2_r.at[src], dev)

    def g3_copy(t, src):
        return remote(piece, gw_ref.at[al(src, per // NZL), :], g3_s.at[t], g3_r.at[src], (t, me))

    frame = frame_ref[...]
    row = lax.broadcasted_iota(jnp.int32, (TAIL, tok), 0)
    digits = jnp.where(row == 0, frame >> 4, jnp.where(row == 1, frame & 15, 0))
    digits = digits.astype(f32).astype(bf)
    for h in range(blocks):
        cols = slice(h * HS, (h + 1) * HS)
        send[h, 0:tok, 0:HS] = q_ref[:, cols]
        send[h, 0:tok, HS : 2 * HS] = k_ref[:, cols]
        send[h, tok : tok + half, 0:HS] = v_ref[0:half, cols]
        send[h, tok : tok + half, HS : 2 * HS] = v_ref[half:tok, cols]
        send[h, tok + half : tok + half + TAIL, :] = digits
    pl.semaphore_wait(barrier, blocks - 1 + dps - 1 + NZH - 1)

    others(NZH, zh, lambda t: w1_copy(t, zh).start())
    others(NY, y, lambda t: cot_copy(t, y).start())
    wp[core, pl.ds(pl.multiple_of((x * NZH + zh) * per, per), per), :] = w_ref[al(y, per), :]
    cotg[al(y, tok), :] = cot_ref[...]
    recv[me] = send[me]

    def near(i, c):
        qkv((me + i) % (2 * NZH) + x * 2 * NZH, me).start()
        return c

    lax.fori_loop(1, 2 * NZH, near, 0)
    others(NZH, zh, lambda t: w1_copy(t, t).wait_recv())
    others(NX, x, lambda t: w2_copy(t, x).start())

    def far(i, c):
        qkv(((x + 1 + i // (2 * NZH)) % NX) * 2 * NZH + (me + i) % (2 * NZH), me).start()
        return c

    lax.fori_loop(0, (NX - 1) * 2 * NZH, far, 0)
    others(NX, x, lambda t: w2_copy(t, t).wait_recv())
    w3_copy(core).start()
    others(NY, y, lambda t: cot_copy(t, t).wait_recv())

    def grad_part(c):
        for b in range(NY):
            part = dg(wp[c], cotg[b * tok : (b + 1) * tok, :], 1, 1).astype(bf)
            dysend[c, b] = part
        others(NY, y, lambda t: dy_copy(c, t, y).start())
        dyrecv[c, y] = dysend[c, y]

    grad_part(core)
    w3_copy(1 - core).wait_recv()
    grad_part(1 - core)
    for c in range(2):
        others(NY, y, lambda t: dy_copy(c, t, t).wait_recv())

    def regroup(i, c):
        t = (me + i) % blocks
        rows = pl.ds(pl.multiple_of((t // 2) * per, per), per)
        for b in range(NY):
            dosend[t, b * per : (b + 1) * per, :] = dyrecv[t % 2, b, rows, :]

        @pl.when(t != me)
        def _():
            do_copy(t, me).start()

        @pl.when(t == me)
        def _():
            dot[:, al(t, tok)] = dosend[t]

        return c

    lax.fori_loop(0, blocks, regroup, 0)
    others(blocks, me, lambda t: qkv(t, t).wait_recv())

    scale = jnp.asarray(HS**-0.5, bf)

    def unpack(t, c):
        first = pl.multiple_of(t * tok, tok)
        qp[pl.ds(first, tok), :] = recv[t, 0:tok, 0:HS] * scale
        kp[pl.ds(first, tok), :] = recv[t, 0:tok, HS : 2 * HS]
        vp[pl.ds(first, half), :] = recv[t, tok : tok + half, 0:HS]
        vp[pl.ds(first + half, half), :] = recv[t, tok : tok + half, HS : 2 * HS]
        dig = recv[t, tok + half : tok + half + TAIL, :].astype(f32)
        fr[0:1, pl.ds(first, tok)] = dig[0:1, :] * 16.0 + dig[1:2, :]
        return c

    lax.fori_loop(0, blocks, unpack, 0)
    kp[length : length + TAIL, :] = jnp.zeros((TAIL, HS), bf)
    vp[length : length + TAIL, :] = jnp.zeros((TAIL, HS), bf)
    fr[0:1, length : length + tok] = jnp.full((1, tok), -1.0, f32)

    def count(t, c):
        first = pl.multiple_of(t * tok, tok)
        wide = fr[0:1, pl.ds(first, 2 * tok)]
        own = wide[:, 0:tok]
        end = lax.broadcasted_iota(jnp.int32, (1, tok), 1) + (first + 1)
        for shift in range(1, TAIL):
            end = end + (wide[:, shift : shift + tok] == own).astype(jnp.int32)
        end_ref[0:1, pl.ds(first, tok)] = end
        return c

    lax.fori_loop(0, blocks, count, 0)

    def score_tile(qh, h, k0, n, end):
        s = dg(kp[pl.ds(k0, n), :], qh, 1, 1)
        if end is not None:
            pos = lax.broadcasted_iota(jnp.int32, (n, QH), 0) + k0
            s = jnp.where(pos < end, s, NEG)
        m = ml[2 * h : 2 * h + 1, :]
        mn = jnp.maximum(m, jnp.max(s, axis=0, keepdims=True))
        p = jnp.exp(s - mn)
        alpha = jnp.exp(m - mn)
        ml[2 * h : 2 * h + 1, :] = mn
        ml[2 * h + 1 : 2 * h + 2, :] = ml[2 * h + 1 : 2 * h + 2, :] * alpha + jnp.sum(
            p, axis=0, keepdims=True
        )
        acc[h] = acc[h] * alpha + dg(vp[pl.ds(k0, n), :], p.astype(bf), 0, 0)

    def qblock(i, c):
        b = (i + me) % steps
        qs = pl.multiple_of(b * QB, QB)
        qh = [qp[pl.ds(qs + h * QH, QH), :] for h in range(2)]
        for h in range(2):
            ml[2 * h : 2 * h + 1, :] = jnp.full((1, QH), NEG, f32)
            ml[2 * h + 1 : 2 * h + 2, :] = jnp.zeros((1, QH), f32)
            acc[h] = jnp.zeros((HS, QH), f32)

        def kb(j, c):
            for h in range(2):
                score_tile(qh[h], h, pl.multiple_of(j * QB, QB), QB, None)
            return c

        lax.fori_loop(0, b, kb, 0)
        for h in range(2):
            score_tile(qh[h], h, qs, (h + 1) * QH + TAIL, end_ref[0:1, pl.ds(qs + h * QH, QH)])
        for h in range(2):
            total = ml[2 * h + 1 : 2 * h + 2, :]
            ot[:, pl.ds(qs + h * QH, QH)] = (acc[h] / total).astype(bf)
            lse_ref[0:1, pl.ds(qs + h * QH, QH)] = ml[2 * h : 2 * h + 1, :] + jnp.log(total)
        for n in range(QB // tok):
            t = (QB // tok) * b + n

            @pl.when(t != me)
            def _():
                o_copy(t, me).start()

            @pl.when(t == me)
            def _():
                orecv[t] = ot[:, al(t, tok)]

        return c

    lax.fori_loop(0, steps, qblock, 0)

    others(blocks, me, lambda t: do_copy(t, t).wait_recv())

    def deltas(t, c):
        cols = al(t, tok)
        prod = dot[:, cols].astype(f32) * ot[:, cols].astype(f32)
        dl[0:1, cols] = jnp.sum(prod, axis=0, keepdims=True)
        return c

    lax.fori_loop(0, blocks, deltas, 0)
    dqt[...] = jnp.zeros_like(dqt)
    others(blocks, me, lambda t: o_copy(t, t).wait_recv())
    for h in range(blocks):
        at = (h % 2) * group + (h // 2) * per
        for b in range(NY):
            aysend[b, at : at + per, :] = orecv[h, b * per : (b + 1) * per, :]
    others(NY, y, lambda t: ay_copy(t, y).start())
    attp[:, al(y, tok)] = aysend[y]

    def tile(k0, n, q0, size, masked):
        qr = pl.ds(q0, size)
        kr = pl.ds(k0, n)
        kk, qh, do = kp[kr, :], qp[qr, :], dot[:, qr]
        p = jnp.exp(dg(kk, qh, 1, 1) - lse_ref[0:1, qr])
        if masked:
            pos = lax.broadcasted_iota(jnp.int32, (n, size), 0) + k0
            p = jnp.where(pos < end_ref[0:1, qr], p, 0.0)
        dp = dg(vp[kr, :], do, 1, 0)
        dva[0:n, :] = dva[0:n, :] + dg(p.astype(bf), do, 1, 1)
        ds = (p * (dp - dl[0:1, qr])).astype(bf)
        dka[0:n, :] = dka[0:n, :] + dg(ds, qh, 1, 0)
        dqt[:, qr] = dqt[:, qr] + dg(kk, ds, 0, 0)

    def kblock(i, c):
        j = (i + me) % steps
        ks = pl.multiple_of(j * QB, QB)
        dka[...] = jnp.zeros_like(dka)
        dva[...] = jnp.zeros_like(dva)

        @pl.when(j > 0)
        def _():
            tile(ks, TAIL, pl.multiple_of(ks - tok, tok), tok, True)

        tile(ks, QH + TAIL, ks, QH, True)
        tile(ks, QB, pl.multiple_of(ks + QH, QH), QH, True)

        def later(b, c):
            qs = pl.multiple_of(b * QB, QB)
            for h in range(2):
                tile(ks, QB, pl.multiple_of(qs + h * QH, QH), QH, False)
            return c

        lax.fori_loop(j + 1, steps, later, 0)
        for n in range(QB // tok):
            t = (QB // tok) * j + n
            kvsend[t, :, 0:HS] = dka[n * tok : (n + 1) * tok, :].astype(bf)
            kvsend[t, :, HS : 2 * HS] = dva[n * tok : (n + 1) * tok, :].astype(bf)
        for n in range(QB // tok):
            t = (QB // tok) * j + n

            @pl.when(t != me)
            def _():
                kv_copy(t, me).start()

            @pl.when(t == me)
            def _():
                kvrecv[t] = kvsend[t]

        @pl.when(i == 1)
        def _():
            others(NY, y, lambda t: ay_copy(t, t).wait_recv())
            for g in range(width // 512):
                cols = slice(g * 512, (g + 1) * 512)
                gwp[:, cols] = dg(attp[...], cotg[:, cols], 1, 0).astype(bf)
            others(2 * NX, xc, lambda t: g1_copy(t, xc).start())

        @pl.when(i == 2)
        def _():
            for b in range(NY):
                mine = attp[:, b * tok : (b + 1) * tok].T
                part = dg(mine[:, 0:group], wp[0], 1, 0) + dg(mine[:, group : 2 * group], wp[1], 1, 0)
                psend[b] = part.astype(bf)
            others(NY, y, lambda t: p_copy(t, y).start())

        @pl.when(i == 5)
        def _():
            others(2 * NX, xc, lambda t: g1_copy(t, t).wait_recv())
            s1recv[xc] = gwp[
                pl.ds(pl.multiple_of(core * group + x * NZH * per, NZH * per), NZH * per), :
            ]
            size = per // NZL
            for n in range(NZH * NZL):
                total = s1recv[0, n * size : (n + 1) * size, :].astype(f32)
                for m in range(1, 2 * NX):
                    total = total + s1recv[m, n * size : (n + 1) * size, :].astype(f32)
                s2send[n] = total.astype(bf)
            others(NZH * NZL, zz, lambda t: g2_copy(t, zz).start())

        return c

    lax.fori_loop(0, steps, kblock, 0)

    def queries_done(i, c):
        t = (i + me) % blocks
        dq = (dqt[:, al(t, tok)] * (HS**-0.5)).T.astype(bf)
        dqsend[t, :, 0:HS] = dq[0:half, :]
        dqsend[t, :, HS : 2 * HS] = dq[half:tok, :]

        @pl.when(t != me)
        def _():
            dq_copy(t, me).start()

        @pl.when(t == me)
        def _():
            dqrecv[t] = dqsend[t]

        return c

    lax.fori_loop(0, blocks, queries_done, 0)

    others(NZH * NZL, zz, lambda t: g2_copy(t, t).wait_recv())
    s2recv[zz] = s2send[zz]
    total = s2recv[0].astype(f32)
    for m in range(1, NZH * NZL):
        total = total + s2recv[m].astype(f32)
    piece[...] = total
    others(dps, d, lambda t: g3_copy(t, d).start())
    gw_ref[al(d, per // NZL), :] = total

    others(NY, y, lambda t: p_copy(t, t).wait_recv())
    precv[y] = psend[y]
    for g in range(width // 512):
        cols = slice(g * 512, (g + 1) * 512)
        total = precv[0, :, cols].astype(f32)
        for b in range(1, NY):
            total = total + precv[b, :, cols].astype(f32)
        out_ref[:, cols] = total.astype(bf)

    others(blocks, me, lambda t: kv_copy(t, t).wait_recv())
    for h in range(blocks):
        cols = slice(h * HS, (h + 1) * HS)
        dk_ref[:, cols] = kvrecv[h, :, 0:HS]
        dv_ref[:, cols] = kvrecv[h, :, HS : 2 * HS]
    others(blocks, me, lambda t: dq_copy(t, t).wait_recv())
    for h in range(blocks):
        cols = slice(h * HS, (h + 1) * HS)
        dq_ref[0:half, cols] = dqrecv[h, :, 0:HS]
        dq_ref[half:tok, cols] = dqrecv[h, :, HS : 2 * HS]
    others(dps, d, lambda t: g3_copy(t, t).wait_recv())

    for mk in (qkv, do_copy, o_copy, kv_copy, dq_copy):
        others(blocks, me, lambda t: mk(t, me).wait_send())
    for mk in (cot_copy, ay_copy, p_copy):
        others(NY, y, lambda t: mk(t, y).wait_send())
    for c in range(2):
        others(NY, y, lambda t: dy_copy(c, t, y).wait_send())
    others(NZH, zh, lambda t: w1_copy(t, zh).wait_send())
    others(NX, x, lambda t: w2_copy(t, x).wait_send())
    w3_copy(core).wait_send()
    others(2 * NX, xc, lambda t: g1_copy(t, xc).wait_send())
    others(NZH * NZL, zz, lambda t: g2_copy(t, zz).wait_send())
    others(dps, d, lambda t: g3_copy(t, d).wait_send())


def on_device(queries, keys, values, frames, out_weight, cotangent):
    tok, width = queries.shape[1], queries.shape[2]
    group = lax.axis_size("seq")
    length = tok * group
    half = tok // 2
    sds = jax.ShapeDtypeStruct
    vmem = pltpu.VMEM
    per = HS // NY

    def sems(*n):
        return [pltpu.SemaphoreType.DMA(n)] * 2

    packed = (group, half, 2 * HS)
    args = (queries[0], keys[0], values[0], frames, cotangent[0], out_weight)
    output, dq, dk, dv, gw = pl.pallas_call(
        kernel,
        out_shape=(sds((tok, width), bf),) * 4 + (sds((HS, width), f32),),
        in_specs=[VM] * len(args),
        out_specs=(VM,) * 5,
        scratch_shapes=[
            vmem((group, tok + half + TAIL, 2 * HS), bf),
            vmem((group, tok + half + TAIL, 2 * HS), bf),
            vmem((length, HS), bf),
            vmem((length + TAIL, HS), bf),
            vmem((length + TAIL, HS), bf),
            vmem((1, length + tok), f32),
            vmem((1, length), jnp.int32),
            vmem((1, length), f32),
            vmem((2, HS, QH), f32),
            vmem((8, QH), f32),
            vmem((2, group // 2 * per, width), bf),
            vmem((NY * tok, width), bf),
            vmem((2, NY, group // 2 * per, tok), bf),
            vmem((2, NY, group // 2 * per, tok), bf),
            vmem((group, HS, tok), bf),
            vmem((HS, length), bf),
            vmem((HS, length), bf),
            vmem((group, HS, tok), bf),
            vmem((NY, group * per, tok), bf),
            vmem((group * per, NY * tok), bf),
            vmem((group, tok, 2 * HS), bf),
            vmem((group, tok, 2 * HS), bf),
            vmem(packed, bf),
            vmem(packed, bf),
            vmem((HS, length), f32),
            vmem((QB, HS), f32),
            vmem((QB, HS), f32),
            vmem((1, length), f32),
            vmem((group * per, width), bf),
            vmem((2 * NX, NZH * per, width), bf),
            vmem((NZH * NZL, per // NZL, width), bf),
            vmem((NZH * NZL, per // NZL, width), bf),
            vmem((per // NZL, width), f32),
            vmem((NY, tok, width), bf),
            vmem((NY, tok, width), bf),
            *sems(group),
            *sems(group),
            *sems(group),
            *sems(group),
            *sems(group),
            *sems(NY),
            *sems(2, NY),
            *sems(NY),
            *sems(NY),
            *sems(NZH),
            *sems(NX),
            *sems(1),
            *sems(2 * NX),
            *sems(NZH * NZL),
            *sems(NY * NZL),
        ],
        compiler_params=pltpu.CompilerParams(
            vmem_limit_bytes=60 << 20, collective_id=0, has_side_effects=True
        ),
        name="attention_step",
    )(*args)
    return output[None], dq[None], dk[None], dv[None], gw


def solution(mesh):
    tokens = P("dp", "seq", None)
    return jax.shard_map(
        on_device,
        mesh=mesh,
        in_specs=(tokens, tokens, tokens, P("dp", "seq"), P("seq", None), tokens),
        out_specs=(tokens, tokens, tokens, tokens, P("seq", None)),
        check_vma=False,
    )
```

```python
import jax
import jax.numpy as jnp
from jax import lax
from jax.experimental import pallas as pl
from jax.experimental.pallas import tpu as pltpu
from jax.sharding import PartitionSpec as P

HS = 64
QB = 512
QH = 256
TAIL = 16
NEG = -1e30
NX, NY, NZH, NZL = 4, 4, 4, 2
f32, bf = jnp.float32, jnp.bfloat16
VM = pl.BlockSpec(memory_space=pltpu.VMEM)
MESH = pl.DeviceIdType.MESH


def dg(a, b, ca, cb):
    return lax.dot_general(a, b, (((ca,), (cb,)), ((), ())), preferred_element_type=f32)


def place():
    d, s = lax.axis_index("dp"), lax.axis_index("seq")
    return d, s


def remote(src, dst, send, recv, device):
    return pltpu.make_async_remote_copy(
        src_ref=src, dst_ref=dst, send_sem=send, recv_sem=recv, device_id=device, device_id_type=MESH
    )


def others(count, me, body):
    def one(i, c):
        body((me + i) % count)
        return c

    lax.fori_loop(1, count, one, 0)


def kernel(
    q_hbm, k_hbm, v_hbm, frame_hbm, cot_hbm, w_hbm,
    sum_ref, kvrecv, dqrecv, gw_ref,
    q_ref, k_ref, v_ref, frame_ref, cot_ref, w_ref, in_s,
    send, recv, qp, kp, vp, fr, end_ref, lse_ref, acc, mx, lx, sall,
    wp, cotg, dysend, dyrecv, dosend, dot, ot, orecv, aysend, attp,
    kvsend, dqsend, dqt, dka, dva, dl,
    gwp, s1recv, s2send, s2recv, piece, psend, precv,
    qkv_s, qkv_r, do_s, do_r, o_s, o_r, kv_s, kv_r, dq_s, dq_r,
    c_s, c_r, dy_s, dy_r, ay_s, ay_r, p_s, p_r,
    w1_s, w1_r, w2_s, w2_r, w3_s, w3_r, g1_s, g1_r, g2_s, g2_r, g3_s, g3_r,
):
    d, me = place()
    y, zl = d // NZL, d % NZL
    x, zh, core = me // (2 * NZH), (me // 2) % NZH, me % 2
    xc, zz = x * 2 + core, zh * NZL + zl
    tok, width = q_ref.shape
    half = tok // 2
    blocks = send.shape[0]
    length = blocks * tok
    steps = length // QB
    per = HS // NY
    group = blocks // 2 * per
    dps = NY * NZL

    def seq_of(xx, zz_, cc):
        return xx * 2 * NZH + zz_ * 2 + cc

    def ydev(t):
        return (t * NZL + zl, me)

    def al(v, n):
        return pl.ds(pl.multiple_of(v * n, n), n)

    def row_of(h):
        return (h % 2) * group + (h // 2) * per

    inputs = [
        pltpu.make_async_copy(a, b, in_s.at[n])
        for n, (a, b) in enumerate(
            (
                (q_hbm, q_ref),
                (k_hbm, k_ref),
                (v_hbm, v_ref),
                (frame_hbm, frame_ref),
                (cot_hbm, cot_ref),
                (w_hbm, w_ref),
            )
        )
    ]
    for copy in inputs:
        copy.start()
    barrier = pltpu.get_barrier_semaphore()

    def greet(dev):
        pl.semaphore_signal(barrier, inc=1, device_id=dev, device_id_type=MESH)

    others(blocks, me, lambda t: greet((d, t)))
    others(dps, d, lambda t: greet((t, me)))
    others(NZH, zh, lambda t: greet((y * NZL + (1 - zl), seq_of(x, t, core))))

    def qkv(t, src):
        return remote(send.at[t], recv.at[src], qkv_s.at[t], qkv_r.at[src], (d, t))

    def cot_copy(t, src):
        return remote(cot_ref, cotg.at[al(src, tok), :], c_s.at[t], c_r.at[src], ydev(t))

    def w1_copy(t, src):
        at = wp.at[core, pl.ds(pl.multiple_of((x * NZH + src) * per, per), per), :]
        return remote(w_ref.at[al(y, per), :], at, w1_s.at[t], w1_r.at[src], (d, seq_of(x, t, core)))

    def w2_copy(t, src):
        own = wp.at[core, al(x, NZH * per), :]
        at = wp.at[core, al(src, NZH * per), :]
        return remote(own, at, w2_s.at[t], w2_r.at[src], (d, seq_of(t, zh, core)))

    def w3_copy(c):
        return remote(wp.at[c], wp.at[c], w3_s.at[0], w3_r.at[0], (d, seq_of(x, zh, 1 - core)))

    def dy_copy(c, t, src):
        return remote(
            dysend.at[c, t], dyrecv.at[c, src], dy_s.at[c, t], dy_r.at[c, src], ydev(t)
        )

    def do_copy(t, src):
        return remote(dosend.at[t], dot.at[:, al(src, tok)], do_s.at[t], do_r.at[src], (d, t))

    def o_copy(t, src):
        return remote(ot.at[:, al(t, tok)], orecv.at[src], o_s.at[t], o_r.at[src], (d, t))

    def ay_copy(t, src):
        return remote(aysend.at[t], attp.at[:, al(src, tok)], ay_s.at[t], ay_r.at[src], ydev(t))

    def p_copy(t, src):
        return remote(psend.at[t], precv.at[src], p_s.at[t], p_r.at[src], ydev(t))

    def kv_copy(t, src):
        return remote(kvsend.at[t], kvrecv.at[src], kv_s.at[t], kv_r.at[src], (d, t))

    def dq_copy(t, src):
        return remote(dqsend.at[t], dqrecv.at[src], dq_s.at[t], dq_r.at[src], (d, t))

    def g1_copy(t, src):
        rows = pl.ds(pl.multiple_of((t % 2) * group + (t // 2) * NZH * per, NZH * per), NZH * per)
        dev = (d, seq_of(t // 2, zh, t % 2))
        return remote(gwp.at[rows, :], s1recv.at[src], g1_s.at[t], g1_r.at[src], dev)

    def g2_copy(t, src):
        dev = (y * NZL + t % NZL, seq_of(x, t // NZL, core))
        return remote(s2send.at[t], s2recv.at[src], g2_s.at[t], g2_r.at[src], dev)

    def g3_copy(t, src):
        return remote(piece, gw_ref.at[al(src, per // NZL), :], g3_s.at[t], g3_r.at[src], (t, me))

    for copy in inputs:
        copy.wait()
    frame = frame_ref[...]
    row = lax.broadcasted_iota(jnp.int32, (TAIL, tok), 0)
    digits = jnp.where(row == 0, frame >> 4, jnp.where(row == 1, frame & 15, 0))
    digits = digits.astype(f32).astype(bf)
    for h in range(blocks):
        cols = slice(h * HS, (h + 1) * HS)
        send[h, 0:tok, 0:HS] = q_ref[:, cols]
        send[h, 0:tok, HS : 2 * HS] = k_ref[:, cols]
        send[h, tok : tok + half, 0:HS] = v_ref[0:half, cols]
        send[h, tok : tok + half, HS : 2 * HS] = v_ref[half:tok, cols]
        send[h, tok + half : tok + half + TAIL, :] = digits
    pl.semaphore_wait(barrier, blocks - 1 + dps - 1 + NZH - 1)

    others(NZH, zh, lambda t: w1_copy(t, zh).start())
    others(NY, y, lambda t: cot_copy(t, y).start())
    wp[core, pl.ds(pl.multiple_of((x * NZH + zh) * per, per), per), :] = w_ref[al(y, per), :]
    cotg[al(y, tok), :] = cot_ref[...]
    recv[me] = send[me]

    def near(i, c):
        qkv((me + i) % (2 * NZH) + x * 2 * NZH, me).start()
        return c

    lax.fori_loop(1, 2 * NZH, near, 0)
    others(NZH, zh, lambda t: w1_copy(t, t).wait_recv())
    others(NX, x, lambda t: w2_copy(t, x).start())

    def far(i, c):
        qkv(((x + 1 + i // (2 * NZH)) % NX) * 2 * NZH + (me + i) % (2 * NZH), me).start()
        return c

    lax.fori_loop(0, (NX - 1) * 2 * NZH, far, 0)
    others(NX, x, lambda t: w2_copy(t, t).wait_recv())
    w3_copy(core).start()
    others(NY, y, lambda t: cot_copy(t, t).wait_recv())

    def grad_part(c):
        for b in range(NY):
            part = dg(wp[c], cotg[b * tok : (b + 1) * tok, :], 1, 1).astype(bf)
            dysend[c, b] = part
        others(NY, y, lambda t: dy_copy(c, t, y).start())
        dyrecv[c, y] = dysend[c, y]

    grad_part(core)
    w3_copy(1 - core).wait_recv()
    grad_part(1 - core)
    scale = jnp.asarray(HS**-0.5, bf)

    def unpack(t):
        first = pl.multiple_of(t * tok, tok)
        qp[pl.ds(first, tok), :] = recv[t, 0:tok, 0:HS] * scale
        kp[pl.ds(first, tok), :] = recv[t, 0:tok, HS : 2 * HS]
        vp[pl.ds(first, half), :] = recv[t, tok : tok + half, 0:HS]
        vp[pl.ds(first + half, half), :] = recv[t, tok : tok + half, HS : 2 * HS]
        dig = recv[t, tok + half : tok + half + TAIL, :].astype(f32)
        fr[pl.ds(t, 1), :] = dig[0:1, :] * 16.0 + dig[1:2, :]

    def near_in(i, c):
        t = (me + i) % (2 * NZH) + x * 2 * NZH
        qkv(t, t).wait_recv()
        unpack(t)
        return c

    def far_in(i, c):
        t = ((x + NX - 1 - i // (2 * NZH)) % NX) * 2 * NZH + (me + i) % (2 * NZH)
        qkv(t, t).wait_recv()
        unpack(t)
        return c

    unpack(me)
    lax.fori_loop(1, 2 * NZH, near_in, 0)
    lax.fori_loop(0, (NX - 1) * 2 * NZH, far_in, 0)
    kp[length : length + TAIL, :] = jnp.zeros((TAIL, HS), bf)
    vp[length : length + TAIL, :] = jnp.zeros((TAIL, HS), bf)
    fr[blocks : blocks + 8, :] = jnp.full((8, tok), -1.0, f32)

    own = fr[0:blocks, :]
    wide = jnp.concatenate([own, fr[1 : blocks + 1, :]], axis=1)
    end = lax.broadcasted_iota(jnp.int32, (blocks, tok), 1) + 1
    end = end + lax.broadcasted_iota(jnp.int32, (blocks, tok), 0) * tok
    for shift in range(1, TAIL):
        end = end + (wide[:, shift : shift + tok] == own).astype(jnp.int32)
    end_ref[...] = end

    def ends(t, size):
        return jnp.concatenate([end_ref[pl.ds(t + n, 1), :] for n in range(size // tok)], axis=1)

    def fold(v, op):
        return op(v.reshape(v.shape[0] // 8, 8, v.shape[1]), axis=0)

    def stat(qh, h, k0, n, end):
        sc = dg(kp[pl.ds(k0, n), :], qh, 1, 1)
        if end is not None:
            pos = lax.broadcasted_iota(jnp.int32, (n, QH), 0) + k0
            sc = jnp.where(pos < end, sc, NEG)
        sall[h, pl.ds(k0, n), :] = sc
        mx[h] = jnp.maximum(mx[h], fold(sc, jnp.max))

    def gather(m, h, k0, n):
        p = jnp.exp(sall[h, pl.ds(k0, n), :] - m)
        lx[h] = lx[h] + fold(p, jnp.sum)
        acc[h] = acc[h] + dg(vp[pl.ds(k0, n), :], p.astype(bf), 0, 0)

    def in_pairs(first, last, body):
        def two(j, c):
            body(first + 2 * j)
            body(first + 2 * j + 1)
            return c

        lax.fori_loop(0, (last - first) // 2, two, 0)

        @pl.when((last - first) % 2 == 1)
        def _():
            body(last - 1)

    def regroup(i, c):
        t = (me + i) % blocks
        rows = pl.ds(pl.multiple_of((t // 2) * per, per), per)
        for b in range(NY):
            dosend[t, b * per : (b + 1) * per, :] = dyrecv[t % 2, b, rows, :]

        @pl.when(t != me)
        def _():
            do_copy(t, me).start()

        @pl.when(t == me)
        def _():
            dot[:, al(t, tok)] = dosend[t]

        return c

    def qblock(i, c):
        b = (i + me) % steps
        qs = pl.multiple_of(b * QB, QB)
        qh = [qp[pl.ds(qs + h * QH, QH), :] for h in range(2)]
        mx[...] = jnp.full_like(mx, NEG)
        lx[...] = jnp.zeros_like(lx)
        acc[...] = jnp.zeros_like(acc)
        for h in range(2):
            stat(qh[h], h, qs, (h + 1) * QH + TAIL, ends((QB // tok) * b + (QH // tok) * h, QH))

        def stats(j):
            for h in range(2):
                stat(qh[h], h, pl.multiple_of(j * QB, QB), QB, None)

        in_pairs(0, b, stats)
        m = [jnp.max(mx[h], axis=0, keepdims=True) for h in range(2)]
        for h in range(2):
            gather(m[h], h, qs, (h + 1) * QH + TAIL)

        def gathers(j):
            for h in range(2):
                gather(m[h], h, pl.multiple_of(j * QB, QB), QB)

        in_pairs(0, b, gathers)
        for h in range(2):
            total = jnp.sum(lx[h], axis=0, keepdims=True)
            ot[:, pl.ds(qs + h * QH, QH)] = (acc[h] / total).astype(bf)
            lse_ref[0:1, pl.ds(qs + h * QH, QH)] = m[h] + jnp.log(total)
        for n in range(QB // tok):
            t = (QB // tok) * b + n

            @pl.when(t != me)
            def _():
                o_copy(t, me).start()

            @pl.when(t == me)
            def _():
                orecv[t] = ot[:, al(t, tok)]

        @pl.when(i == 0)
        def _():
            for c in range(2):
                others(NY, y, lambda t: dy_copy(c, t, t).wait_recv())
            lax.fori_loop(0, blocks, regroup, 0)

        return c

    lax.fori_loop(0, steps, qblock, 0)

    others(blocks, me, lambda t: do_copy(t, t).wait_recv())

    def deltas(t, c):
        cols = al(t, tok)
        prod = dot[:, cols].astype(f32) * ot[:, cols].astype(f32)
        dl[0:1, cols] = jnp.sum(prod, axis=0, keepdims=True)
        return c

    lax.fori_loop(0, blocks, deltas, 0)
    dqt[...] = jnp.zeros_like(dqt)

    def tile(k0, n, q0, size, end):
        qr = pl.ds(q0, size)
        kr = pl.ds(k0, n)
        kk, qh, do = kp[kr, :], qp[qr, :], dot[:, qr]
        p = jnp.exp(dg(kk, qh, 1, 1) - lse_ref[0:1, qr])
        if end is not None:
            pos = lax.broadcasted_iota(jnp.int32, (n, size), 0) + k0
            p = jnp.where(pos < end, p, 0.0)
        dp = dg(vp[kr, :], do, 1, 0)
        dva[0:n, :] = dva[0:n, :] + dg(p.astype(bf), do, 1, 1)
        ds = (p * (dp - dl[0:1, qr])).astype(bf)
        dka[0:n, :] = dka[0:n, :] + dg(ds, qh, 1, 0)
        dqt[:, qr] = dqt[:, qr] + dg(kk, ds, 0, 0)

    def kblock(i, c):
        j = (i + me) % steps
        ks = pl.multiple_of(j * QB, QB)
        first = (QB // tok) * j
        dka[...] = jnp.zeros_like(dka)
        dva[...] = jnp.zeros_like(dva)

        @pl.when(j > 0)
        def _():
            tile(ks, TAIL, pl.multiple_of(ks - tok, tok), tok, ends(first - 1, tok))

        tile(ks, QH + TAIL, ks, QH, ends(first, QH))
        tile(ks, QB, pl.multiple_of(ks + QH, QH), QH, ends(first + QH // tok, QH))

        def later(b):
            qs = pl.multiple_of(b * QB, QB)
            for h in range(2):
                tile(ks, QB, pl.multiple_of(qs + h * QH, QH), QH, None)

        in_pairs(j + 1, steps, later)
        for n in range(QB // tok):
            t = (QB // tok) * j + n
            kvsend[t, :, 0:HS] = dka[n * tok : (n + 1) * tok, :].astype(bf)
            kvsend[t, :, HS : 2 * HS] = dva[n * tok : (n + 1) * tok, :].astype(bf)
        for n in range(QB // tok):
            t = (QB // tok) * j + n

            @pl.when(t != me)
            def _():
                kv_copy(t, me).start()

            @pl.when(t == me)
            def _():
                kvrecv[t] = kvsend[t]

        @pl.when(i == 0)
        def _():
            others(blocks, me, lambda t: o_copy(t, t).wait_recv())
            for h in range(blocks):
                at = (h % 2) * group + (h // 2) * per
                for b in range(NY):
                    aysend[b, at : at + per, :] = orecv[h, b * per : (b + 1) * per, :]
            others(NY, y, lambda t: ay_copy(t, y).start())
            attp[:, al(y, tok)] = aysend[y]

        @pl.when(i == 1)
        def _():
            others(NY, y, lambda t: ay_copy(t, t).wait_recv())
            for g in range(width // 512):
                cols = slice(g * 512, (g + 1) * 512)
                gwp[:, cols] = dg(attp[...], cotg[:, cols], 1, 0).astype(bf)
            others(2 * NX, xc, lambda t: g1_copy(t, xc).start())

        @pl.when(i == 2)
        def _():
            for b in range(NY):
                mine = attp[:, b * tok : (b + 1) * tok].T
                part = dg(mine[:, 0:group], wp[0], 1, 0) + dg(mine[:, group : 2 * group], wp[1], 1, 0)
                psend[b] = part.astype(bf)
            others(NY, y, lambda t: p_copy(t, y).start())

        @pl.when(i == 5)
        def _():
            others(2 * NX, xc, lambda t: g1_copy(t, t).wait_recv())
            s1recv[xc] = gwp[
                pl.ds(pl.multiple_of(core * group + x * NZH * per, NZH * per), NZH * per), :
            ]
            size = per // NZL
            for n in range(NZH * NZL):
                total = s1recv[0, n * size : (n + 1) * size, :].astype(f32)
                for m in range(1, 2 * NX):
                    total = total + s1recv[m, n * size : (n + 1) * size, :].astype(f32)
                s2send[n] = total.astype(bf)
            others(NZH * NZL, zz, lambda t: g2_copy(t, zz).start())

        return c

    lax.fori_loop(0, steps, kblock, 0)

    def queries_done(i, c):
        t = (i + me) % blocks
        dq = (dqt[:, al(t, tok)] * (HS**-0.5)).T.astype(bf)
        dqsend[t, :, 0:HS] = dq[0:half, :]
        dqsend[t, :, HS : 2 * HS] = dq[half:tok, :]

        @pl.when(t != me)
        def _():
            dq_copy(t, me).start()

        @pl.when(t == me)
        def _():
            dqrecv[t] = dqsend[t]

        return c

    lax.fori_loop(0, blocks, queries_done, 0)

    others(NZH * NZL, zz, lambda t: g2_copy(t, t).wait_recv())
    s2recv[zz] = s2send[zz]
    total = s2recv[0].astype(f32)
    for m in range(1, NZH * NZL):
        total = total + s2recv[m].astype(f32)
    piece[...] = total
    others(dps, d, lambda t: g3_copy(t, d).start())
    gw_ref[al(d, per // NZL), :] = total

    others(NY, y, lambda t: p_copy(t, t).wait_recv())
    precv[y] = psend[y]
    for g in range(width // 512):
        cols = slice(g * 512, (g + 1) * 512)
        total = precv[0, :, cols].astype(f32)
        for b in range(1, NY):
            total = total + precv[b, :, cols].astype(f32)
        sum_ref[:, cols] = total.astype(bf)
    others(blocks, me, lambda t: kv_copy(t, t).wait_recv())
    others(blocks, me, lambda t: dq_copy(t, t).wait_recv())
    others(dps, d, lambda t: g3_copy(t, t).wait_recv())

    for mk in (qkv, do_copy, o_copy, kv_copy, dq_copy):
        others(blocks, me, lambda t: mk(t, me).wait_send())
    for mk in (cot_copy, ay_copy, p_copy):
        others(NY, y, lambda t: mk(t, y).wait_send())
    for c in range(2):
        others(NY, y, lambda t: dy_copy(c, t, y).wait_send())
    others(NZH, zh, lambda t: w1_copy(t, zh).wait_send())
    others(NX, x, lambda t: w2_copy(t, x).wait_send())
    w3_copy(core).wait_send()
    others(2 * NX, xc, lambda t: g1_copy(t, xc).wait_send())
    others(NZH * NZL, zz, lambda t: g2_copy(t, zz).wait_send())
    others(dps, d, lambda t: g3_copy(t, d).wait_send())


def finish_kernel(out_in, kvrecv, dqrecv, gw_in, out_ref, dq_ref, dk_ref, dv_ref, gw_ref):
    tok, width = out_ref.shape
    half = tok // 2
    gw_ref[...] = gw_in[...]
    out_ref[...] = out_in[...]
    for h in range(kvrecv.shape[0]):
        cols = slice(h * HS, (h + 1) * HS)
        dk_ref[:, cols] = kvrecv[h, :, 0:HS]
        dv_ref[:, cols] = kvrecv[h, :, HS : 2 * HS]
        dq_ref[0:half, cols] = dqrecv[h, :, 0:HS]
        dq_ref[half:tok, cols] = dqrecv[h, :, HS : 2 * HS]


def on_device(queries, keys, values, frames, out_weight, cotangent):
    tok, width = queries.shape[1], queries.shape[2]
    group = lax.axis_size("seq")
    length = tok * group
    half = tok // 2
    sds = jax.ShapeDtypeStruct
    vmem = pltpu.VMEM
    per = HS // NY

    def sems(*n):
        return [pltpu.SemaphoreType.DMA(n)] * 2

    packed = (group, half, 2 * HS)
    args = (queries[0], keys[0], values[0], frames, cotangent[0], out_weight)
    received = pl.pallas_call(
        kernel,
        out_shape=(
            sds((tok, width), bf),
            sds((group, tok, 2 * HS), bf),
            sds(packed, bf),
            sds((HS, width), f32),
        ),
        in_specs=[pl.BlockSpec(memory_space=pltpu.HBM)] * len(args),
        out_specs=(VM,) * 4,
        scratch_shapes=[
            vmem((tok, width), bf),
            vmem((tok, width), bf),
            vmem((tok, width), bf),
            vmem((1, tok), jnp.int32),
            vmem((tok, width), bf),
            vmem((HS, width), bf),
            pltpu.SemaphoreType.DMA((6,)),
            vmem((group, tok + half + TAIL, 2 * HS), bf),
            vmem((group, tok + half + TAIL, 2 * HS), bf),
            vmem((length, HS), bf),
            vmem((length + TAIL, HS), bf),
            vmem((length + TAIL, HS), bf),
            vmem((group + 8, tok), f32),
            vmem((group, tok), jnp.int32),
            vmem((1, length), f32),
            vmem((2, HS, QH), f32),
            vmem((2, 8, QH), f32),
            vmem((2, 8, QH), f32),
            vmem((2, length + TAIL, QH), f32),
            vmem((2, group // 2 * per, width), bf),
            vmem((NY * tok, width), bf),
            vmem((2, NY, group // 2 * per, tok), bf),
            vmem((2, NY, group // 2 * per, tok), bf),
            vmem((group, HS, tok), bf),
            vmem((HS, length), bf),
            vmem((HS, length), bf),
            vmem((group, HS, tok), bf),
            vmem((NY, group * per, tok), bf),
            vmem((group * per, NY * tok), bf),
            vmem((group, tok, 2 * HS), bf),
            vmem(packed, bf),
            vmem((HS, length), f32),
            vmem((QB, HS), f32),
            vmem((QB, HS), f32),
            vmem((1, length), f32),
            vmem((group * per, width), bf),
            vmem((2 * NX, NZH * per, width), bf),
            vmem((NZH * NZL, per // NZL, width), bf),
            vmem((NZH * NZL, per // NZL, width), bf),
            vmem((per // NZL, width), f32),
            vmem((NY, tok, width), bf),
            vmem((NY, tok, width), bf),
            *sems(group),
            *sems(group),
            *sems(group),
            *sems(group),
            *sems(group),
            *sems(NY),
            *sems(2, NY),
            *sems(NY),
            *sems(NY),
            *sems(NZH),
            *sems(NX),
            *sems(1),
            *sems(2 * NX),
            *sems(NZH * NZL),
            *sems(NY * NZL),
        ],
        compiler_params=pltpu.CompilerParams(
            vmem_limit_bytes=59 << 20, collective_id=0, has_side_effects=True
        ),
        name="attention_step",
    )(*args)
    output, dq, dk, dv, gw = pl.pallas_call(
        finish_kernel,
        out_shape=(sds((tok, width), bf),) * 4 + (sds((HS, width), f32),),
        in_specs=[VM] * 4,
        out_specs=(VM,) * 5,
        compiler_params=pltpu.CompilerParams(vmem_limit_bytes=60 << 20),
        name="finish",
    )(*received)
    return output[None], dq[None], dk[None], dv[None], gw


def solution(mesh):
    tokens = P("dp", "seq", None)
    return jax.shard_map(
        on_device,
        mesh=mesh,
        in_specs=(tokens, tokens, tokens, P("dp", "seq"), P("seq", None), tokens),
        out_specs=(tokens, tokens, tokens, tokens, P("seq", None)),
        check_vma=False,
    )
```

```python
import jax
import jax.numpy as jnp
from jax import lax
from jax.experimental import pallas as pl
from jax.experimental.pallas import tpu as pltpu
from jax.sharding import PartitionSpec as P

HS = 64
QB = 512
QH = 256
TAIL = 16
NEG = -1e30
NX, NY, NZH, NZL = 4, 4, 4, 2
f32, bf = jnp.float32, jnp.bfloat16
VM = pl.BlockSpec(memory_space=pltpu.VMEM)
MESH = pl.DeviceIdType.MESH


def dg(a, b, ca, cb):
    return lax.dot_general(a, b, (((ca,), (cb,)), ((), ())), preferred_element_type=f32)


def place():
    d, s = lax.axis_index("dp"), lax.axis_index("seq")
    return d, s


def remote(src, dst, send, recv, device):
    return pltpu.make_async_remote_copy(
        src_ref=src, dst_ref=dst, send_sem=send, recv_sem=recv, device_id=device, device_id_type=MESH
    )


def others(count, me, body):
    def one(i, c):
        body((me + i) % count)
        return c

    lax.fori_loop(1, count, one, 0)


def kernel(
    q_hbm, k_hbm, v_hbm, frame_hbm, cot_hbm, w_hbm,
    sum_ref, kvrecv, dqrecv, gw_ref,
    q_ref, k_ref, v_ref, frame_ref, cot_ref, w_ref, in_s,
    send, recv, qp, kp, vp, fr, end_ref, lse_ref, acc, mx, lx, sall,
    wp, cotg, dysend, dyrecv, dosend, dot, ot, orecv, aysend, attp,
    kvsend, dqsend, dqt, dka, dva, dl,
    gwp, s0recv, s1recv, s2send, s2recv, piece, psend, precv,
    qkv_s, qkv_r, do_s, do_r, o_s, o_r, kv_s, kv_r, dq_s, dq_r,
    c_s, c_r, dy_s, dy_r, ay_s, ay_r, p_s, p_r,
    w1_s, w1_r, w2_s, w2_r, w3_s, w3_r, g0_s, g0_r, g1_s, g1_r, g2_s, g2_r, g3_s, g3_r,
):
    d, me = place()
    y, zl = d // NZL, d % NZL
    x, zh, core = me // (2 * NZH), (me // 2) % NZH, me % 2
    zz = zh * NZL + zl
    tok, width = q_ref.shape
    half = tok // 2
    blocks = send.shape[0]
    length = blocks * tok
    steps = length // QB
    per = HS // NY
    group = blocks // 2 * per
    dps = NY * NZL

    def seq_of(xx, zz_, cc):
        return xx * 2 * NZH + zz_ * 2 + cc

    def ydev(t):
        return (t * NZL + zl, me)

    def al(v, n):
        return pl.ds(pl.multiple_of(v * n, n), n)

    def row_of(h):
        return (h % 2) * group + (h // 2) * per

    inputs = [
        pltpu.make_async_copy(a, b, in_s.at[n])
        for n, (a, b) in enumerate(
            (
                (q_hbm, q_ref),
                (k_hbm, k_ref),
                (v_hbm, v_ref),
                (frame_hbm, frame_ref),
                (cot_hbm, cot_ref),
                (w_hbm, w_ref),
            )
        )
    ]
    for copy in inputs:
        copy.start()
    barrier = pltpu.get_barrier_semaphore()

    def greet(dev):
        pl.semaphore_signal(barrier, inc=1, device_id=dev, device_id_type=MESH)

    others(blocks, me, lambda t: greet((d, t)))
    others(dps, d, lambda t: greet((t, me)))
    others(NZH, zh, lambda t: greet((y * NZL + (1 - zl), seq_of(x, t, core))))

    def qkv(t, src):
        return remote(send.at[t], recv.at[src], qkv_s.at[t], qkv_r.at[src], (d, t))

    def cot_copy(t, src):
        return remote(cot_ref, cotg.at[al(src, tok), :], c_s.at[t], c_r.at[src], ydev(t))

    def w1_copy(t, src):
        at = wp.at[core, pl.ds(pl.multiple_of((x * NZH + src) * per, per), per), :]
        return remote(w_ref.at[al(y, per), :], at, w1_s.at[t], w1_r.at[src], (d, seq_of(x, t, core)))

    def w2_copy(t, src):
        own = wp.at[core, al(x, NZH * per), :]
        at = wp.at[core, al(src, NZH * per), :]
        return remote(own, at, w2_s.at[t], w2_r.at[src], (d, seq_of(t, zh, core)))

    def w3_copy(c):
        return remote(wp.at[c], wp.at[c], w3_s.at[0], w3_r.at[0], (d, seq_of(x, zh, 1 - core)))

    def dy_copy(c, t, src):
        return remote(
            dysend.at[c, t], dyrecv.at[c, src], dy_s.at[c, t], dy_r.at[c, src], ydev(t)
        )

    def do_copy(t, src):
        return remote(dosend.at[t], dot.at[:, al(src, tok)], do_s.at[t], do_r.at[src], (d, t))

    def o_copy(t, src):
        return remote(ot.at[:, al(t, tok)], orecv.at[src], o_s.at[t], o_r.at[src], (d, t))

    def ay_copy(t, src):
        return remote(aysend.at[t], attp.at[:, al(src, tok)], ay_s.at[t], ay_r.at[src], ydev(t))

    def p_copy(t, src):
        return remote(psend.at[t], precv.at[src], p_s.at[t], p_r.at[src], ydev(t))

    def kv_copy(t, src):
        return remote(kvsend.at[t], kvrecv.at[src], kv_s.at[t], kv_r.at[src], (d, t))

    def dq_copy(t, src):
        return remote(dqsend.at[t], dqrecv.at[src], dq_s.at[t], dq_r.at[src], (d, t))

    def g0_copy(c):
        return remote(gwp.at[al(c, group), :], s0recv, g0_s.at[0], g0_r.at[0], (d, seq_of(x, zh, 1 - core)))

    def g1_copy(t, src):
        rows = pl.ds(pl.multiple_of(core * group + t * NZH * per, NZH * per), NZH * per)
        dev = (d, seq_of(t, zh, core))
        return remote(gwp.at[rows, :], s1recv.at[src], g1_s.at[t], g1_r.at[src], dev)

    def g2_copy(t, src):
        dev = (y * NZL + t % NZL, seq_of(x, t // NZL, core))
        return remote(s2send.at[t], s2recv.at[src], g2_s.at[t], g2_r.at[src], dev)

    def g3_copy(t, src):
        return remote(piece, gw_ref.at[al(src, per // NZL), :], g3_s.at[t], g3_r.at[src], (t, me))

    for copy in inputs:
        copy.wait()
    frame = frame_ref[...]
    row = lax.broadcasted_iota(jnp.int32, (TAIL, tok), 0)
    digits = jnp.where(row == 0, frame >> 4, jnp.where(row == 1, frame & 15, 0))
    digits = digits.astype(f32).astype(bf)
    for h in range(blocks):
        cols = slice(h * HS, (h + 1) * HS)
        send[h, 0:tok, 0:HS] = q_ref[:, cols]
        send[h, 0:tok, HS : 2 * HS] = k_ref[:, cols]
        send[h, tok : tok + half, 0:HS] = v_ref[0:half, cols]
        send[h, tok : tok + half, HS : 2 * HS] = v_ref[half:tok, cols]
        send[h, tok + half : tok + half + TAIL, :] = digits
    pl.semaphore_wait(barrier, blocks - 1 + dps - 1 + NZH - 1)

    others(NZH, zh, lambda t: w1_copy(t, zh).start())
    others(NY, y, lambda t: cot_copy(t, y).start())
    wp[core, pl.ds(pl.multiple_of((x * NZH + zh) * per, per), per), :] = w_ref[al(y, per), :]
    cotg[al(y, tok), :] = cot_ref[...]
    recv[me] = send[me]

    def near(i, c):
        qkv((me + i) % (2 * NZH) + x * 2 * NZH, me).start()
        return c

    lax.fori_loop(1, 2 * NZH, near, 0)
    others(NZH, zh, lambda t: w1_copy(t, t).wait_recv())
    others(NX, x, lambda t: w2_copy(t, x).start())

    def far(i, c):
        qkv(((x + 1 + i // (2 * NZH)) % NX) * 2 * NZH + (me + i) % (2 * NZH), me).start()
        return c

    lax.fori_loop(0, (NX - 1) * 2 * NZH, far, 0)
    others(NX, x, lambda t: w2_copy(t, t).wait_recv())
    w3_copy(core).start()
    others(NY, y, lambda t: cot_copy(t, t).wait_recv())

    def grad_part(c):
        for b in range(NY):
            part = dg(wp[c], cotg[b * tok : (b + 1) * tok, :], 1, 1).astype(bf)
            dysend[c, b] = part
        others(NY, y, lambda t: dy_copy(c, t, y).start())
        dyrecv[c, y] = dysend[c, y]

    grad_part(core)
    w3_copy(1 - core).wait_recv()
    grad_part(1 - core)
    scale = jnp.asarray(HS**-0.5, bf)

    def unpack(t):
        first = pl.multiple_of(t * tok, tok)
        qp[pl.ds(first, tok), :] = recv[t, 0:tok, 0:HS] * scale
        kp[pl.ds(first, tok), :] = recv[t, 0:tok, HS : 2 * HS]
        vp[pl.ds(first, half), :] = recv[t, tok : tok + half, 0:HS]
        vp[pl.ds(first + half, half), :] = recv[t, tok : tok + half, HS : 2 * HS]
        dig = recv[t, tok + half : tok + half + TAIL, :].astype(f32)
        fr[pl.ds(t, 1), :] = dig[0:1, :] * 16.0 + dig[1:2, :]

    def near_in(i, c):
        t = (me + i) % (2 * NZH) + x * 2 * NZH
        qkv(t, t).wait_recv()
        unpack(t)
        return c

    def far_in(i, c):
        t = ((x + NX - 1 - i // (2 * NZH)) % NX) * 2 * NZH + (me + i) % (2 * NZH)
        qkv(t, t).wait_recv()
        unpack(t)
        return c

    def regroup(i, c):
        t = (me + i) % blocks
        rows = pl.ds(pl.multiple_of((t // 2) * per, per), per)
        for b in range(NY):
            dosend[t, b * per : (b + 1) * per, :] = dyrecv[t % 2, b, rows, :]

        @pl.when(t != me)
        def _():
            do_copy(t, me).start()

        @pl.when(t == me)
        def _():
            dot[:, al(t, tok)] = dosend[t]

        return c

    for c in range(2):
        others(NY, y, lambda t: dy_copy(c, t, t).wait_recv())
    lax.fori_loop(0, blocks, regroup, 0)
    unpack(me)
    lax.fori_loop(1, 2 * NZH, near_in, 0)
    lax.fori_loop(0, (NX - 1) * 2 * NZH, far_in, 0)
    kp[length : length + TAIL, :] = jnp.zeros((TAIL, HS), bf)
    vp[length : length + TAIL, :] = jnp.zeros((TAIL, HS), bf)
    fr[blocks : blocks + 8, :] = jnp.full((8, tok), -1.0, f32)

    own = fr[0:blocks, :]
    wide = jnp.concatenate([own, fr[1 : blocks + 1, :]], axis=1)
    end = lax.broadcasted_iota(jnp.int32, (blocks, tok), 1) + 1
    end = end + lax.broadcasted_iota(jnp.int32, (blocks, tok), 0) * tok
    for shift in range(1, TAIL):
        end = end + (wide[:, shift : shift + tok] == own).astype(jnp.int32)
    end_ref[...] = end

    def ends(t, size):
        return jnp.concatenate([end_ref[pl.ds(t + n, 1), :] for n in range(size // tok)], axis=1)

    def fold(v, op):
        return op(v.reshape(v.shape[0] // 8, 8, v.shape[1]), axis=0)

    def stat(qh, h, k0, n, end):
        sc = dg(kp[pl.ds(k0, n), :], qh, 1, 1)
        if end is not None:
            pos = lax.broadcasted_iota(jnp.int32, (n, QH), 0) + k0
            sc = jnp.where(pos < end, sc, NEG)
        sall[h, pl.ds(k0, n), :] = sc
        mx[h] = jnp.maximum(mx[h], fold(sc, jnp.max))

    def gather(m, h, k0, n):
        p = jnp.exp(sall[h, pl.ds(k0, n), :] - m)
        lx[h] = lx[h] + fold(p, jnp.sum)
        acc[h] = acc[h] + dg(vp[pl.ds(k0, n), :], p.astype(bf), 0, 0)

    def in_pairs(first, last, body):
        def two(j, c):
            body(first + 2 * j)
            body(first + 2 * j + 1)
            return c

        lax.fori_loop(0, (last - first) // 2, two, 0)

        @pl.when((last - first) % 2 == 1)
        def _():
            body(last - 1)

    def qblock(i, c):
        b = (i + me) % steps
        qs = pl.multiple_of(b * QB, QB)
        qh = [qp[pl.ds(qs + h * QH, QH), :] for h in range(2)]
        mx[...] = jnp.full_like(mx, NEG)
        lx[...] = jnp.zeros_like(lx)
        acc[...] = jnp.zeros_like(acc)
        for h in range(2):
            stat(qh[h], h, qs, (h + 1) * QH + TAIL, ends((QB // tok) * b + (QH // tok) * h, QH))

        def stats(j):
            for h in range(2):
                stat(qh[h], h, pl.multiple_of(j * QB, QB), QB, None)

        in_pairs(0, b, stats)
        m = [jnp.max(mx[h], axis=0, keepdims=True) for h in range(2)]
        for h in range(2):
            gather(m[h], h, qs, (h + 1) * QH + TAIL)

        def gathers(j):
            for h in range(2):
                gather(m[h], h, pl.multiple_of(j * QB, QB), QB)

        in_pairs(0, b, gathers)
        for h in range(2):
            total = jnp.sum(lx[h], axis=0, keepdims=True)
            ot[:, pl.ds(qs + h * QH, QH)] = (acc[h] / total).astype(bf)
            lse_ref[0:1, pl.ds(qs + h * QH, QH)] = m[h] + jnp.log(total)
        for n in range(QB // tok):
            t = (QB // tok) * b + n

            @pl.when(t != me)
            def _():
                o_copy(t, me).start()

            @pl.when(t == me)
            def _():
                orecv[t] = ot[:, al(t, tok)]

        return c

    lax.fori_loop(0, steps, qblock, 0)

    others(blocks, me, lambda t: do_copy(t, t).wait_recv())

    def deltas(t, c):
        cols = al(t, tok)
        prod = dot[:, cols].astype(f32) * ot[:, cols].astype(f32)
        dl[0:1, cols] = jnp.sum(prod, axis=0, keepdims=True)
        return c

    lax.fori_loop(0, blocks, deltas, 0)
    dqt[...] = jnp.zeros_like(dqt)

    def tile(k0, n, q0, size, end):
        qr = pl.ds(q0, size)
        kr = pl.ds(k0, n)
        kk, qh, do = kp[kr, :], qp[qr, :], dot[:, qr]
        p = jnp.exp(dg(kk, qh, 1, 1) - lse_ref[0:1, qr])
        if end is not None:
            pos = lax.broadcasted_iota(jnp.int32, (n, size), 0) + k0
            p = jnp.where(pos < end, p, 0.0)
        dp = dg(vp[kr, :], do, 1, 0)
        dva[0:n, :] = dva[0:n, :] + dg(p.astype(bf), do, 1, 1)
        ds = (p * (dp - dl[0:1, qr])).astype(bf)
        dka[0:n, :] = dka[0:n, :] + dg(ds, qh, 1, 0)
        dqt[:, qr] = dqt[:, qr] + dg(kk, ds, 0, 0)

    def kblock(i, c):
        j = (i + me) % steps
        ks = pl.multiple_of(j * QB, QB)
        first = (QB // tok) * j
        dka[...] = jnp.zeros_like(dka)
        dva[...] = jnp.zeros_like(dva)

        @pl.when(j > 0)
        def _():
            tile(ks, TAIL, pl.multiple_of(ks - tok, tok), tok, ends(first - 1, tok))

        tile(ks, QH + TAIL, ks, QH, ends(first, QH))
        tile(ks, QB, pl.multiple_of(ks + QH, QH), QH, ends(first + QH // tok, QH))

        def later(b):
            qs = pl.multiple_of(b * QB, QB)
            for h in range(2):
                tile(ks, QB, pl.multiple_of(qs + h * QH, QH), QH, None)

        in_pairs(j + 1, steps, later)
        for n in range(QB // tok):
            t = (QB // tok) * j + n
            kvsend[t, :, 0:HS] = dka[n * tok : (n + 1) * tok, :].astype(bf)
            kvsend[t, :, HS : 2 * HS] = dva[n * tok : (n + 1) * tok, :].astype(bf)
        for n in range(QB // tok):
            t = (QB // tok) * j + n

            @pl.when(t != me)
            def _():
                kv_copy(t, me).start()

            @pl.when(t == me)
            def _():
                kvrecv[t] = kvsend[t]

        @pl.when(i == 0)
        def _():
            others(blocks, me, lambda t: o_copy(t, t).wait_recv())
            for h in range(blocks):
                at = (h % 2) * group + (h // 2) * per
                for b in range(NY):
                    aysend[b, at : at + per, :] = orecv[h, b * per : (b + 1) * per, :]
            others(NY, y, lambda t: ay_copy(t, y).start())
            attp[:, al(y, tok)] = aysend[y]

        @pl.when(i == 1)
        def _():
            others(NY, y, lambda t: ay_copy(t, t).wait_recv())
            for g in range(width // 512):
                cols = slice(g * 512, (g + 1) * 512)
                gwp[:, cols] = dg(attp[...], cotg[:, cols], 1, 0).astype(bf)
            g0_copy(1 - core).start()
            g0_copy(1 - core).wait_recv()
            for n in range(group // 32):
                rows = pl.ds(pl.multiple_of(core * group + n * 32, 32), 32)
                both = gwp[rows, :].astype(f32) + s0recv[n * 32 : (n + 1) * 32, :].astype(f32)
                gwp[rows, :] = both.astype(bf)
            others(NX, x, lambda t: g1_copy(t, x).start())

        @pl.when(i == 2)
        def _():
            for b in range(NY):
                mine = attp[:, b * tok : (b + 1) * tok].T
                part = dg(mine[:, 0:group], wp[0], 1, 0) + dg(mine[:, group : 2 * group], wp[1], 1, 0)
                psend[b] = part.astype(bf)
            others(NY, y, lambda t: p_copy(t, y).start())

        @pl.when(i == 4)
        def _():
            others(NX, x, lambda t: g1_copy(t, t).wait_recv())
            s1recv[x] = gwp[
                pl.ds(pl.multiple_of(core * group + x * NZH * per, NZH * per), NZH * per), :
            ]
            size = per // NZL
            for n in range(NZH * NZL):
                total = s1recv[0, n * size : (n + 1) * size, :].astype(f32)
                for m in range(1, NX):
                    total = total + s1recv[m, n * size : (n + 1) * size, :].astype(f32)
                s2send[n] = total.astype(bf)
            others(NZH * NZL, zz, lambda t: g2_copy(t, zz).start())

        return c

    lax.fori_loop(0, steps, kblock, 0)

    def queries_done(i, c):
        t = (i + me) % blocks
        dq = (dqt[:, al(t, tok)] * (HS**-0.5)).T.astype(bf)
        dqsend[t, :, 0:HS] = dq[0:half, :]
        dqsend[t, :, HS : 2 * HS] = dq[half:tok, :]

        @pl.when(t != me)
        def _():
            dq_copy(t, me).start()

        @pl.when(t == me)
        def _():
            dqrecv[t] = dqsend[t]

        return c

    lax.fori_loop(0, blocks, queries_done, 0)

    others(NZH * NZL, zz, lambda t: g2_copy(t, t).wait_recv())
    s2recv[zz] = s2send[zz]
    total = s2recv[0].astype(f32)
    for m in range(1, NZH * NZL):
        total = total + s2recv[m].astype(f32)
    piece[...] = total
    others(dps, d, lambda t: g3_copy(t, d).start())
    gw_ref[al(d, per // NZL), :] = total

    others(NY, y, lambda t: p_copy(t, t).wait_recv())
    precv[y] = psend[y]
    for g in range(width // 512):
        cols = slice(g * 512, (g + 1) * 512)
        total = precv[0, :, cols].astype(f32)
        for b in range(1, NY):
            total = total + precv[b, :, cols].astype(f32)
        sum_ref[:, cols] = total.astype(bf)
    others(blocks, me, lambda t: kv_copy(t, t).wait_recv())
    others(blocks, me, lambda t: dq_copy(t, t).wait_recv())
    others(dps, d, lambda t: g3_copy(t, t).wait_recv())

    for mk in (qkv, do_copy, o_copy, kv_copy, dq_copy):
        others(blocks, me, lambda t: mk(t, me).wait_send())
    for mk in (cot_copy, ay_copy, p_copy):
        others(NY, y, lambda t: mk(t, y).wait_send())
    for c in range(2):
        others(NY, y, lambda t: dy_copy(c, t, y).wait_send())
    others(NZH, zh, lambda t: w1_copy(t, zh).wait_send())
    others(NX, x, lambda t: w2_copy(t, x).wait_send())
    w3_copy(core).wait_send()
    g0_copy(1 - core).wait_send()
    others(NX, x, lambda t: g1_copy(t, x).wait_send())
    others(NZH * NZL, zz, lambda t: g2_copy(t, zz).wait_send())
    others(dps, d, lambda t: g3_copy(t, d).wait_send())


def finish_kernel(out_in, kvrecv, dqrecv, gw_in, out_ref, dq_ref, dk_ref, dv_ref, gw_ref):
    tok, width = out_ref.shape
    half = tok // 2
    gw_ref[...] = gw_in[...]
    out_ref[...] = out_in[...]
    for h in range(kvrecv.shape[0]):
        cols = slice(h * HS, (h + 1) * HS)
        dk_ref[:, cols] = kvrecv[h, :, 0:HS]
        dv_ref[:, cols] = kvrecv[h, :, HS : 2 * HS]
        dq_ref[0:half, cols] = dqrecv[h, :, 0:HS]
        dq_ref[half:tok, cols] = dqrecv[h, :, HS : 2 * HS]


def on_device(queries, keys, values, frames, out_weight, cotangent):
    tok, width = queries.shape[1], queries.shape[2]
    group = lax.axis_size("seq")
    length = tok * group
    half = tok // 2
    sds = jax.ShapeDtypeStruct
    vmem = pltpu.VMEM
    per = HS // NY

    def sems(*n):
        return [pltpu.SemaphoreType.DMA(n)] * 2

    packed = (group, half, 2 * HS)
    args = (queries[0], keys[0], values[0], frames, cotangent[0], out_weight)
    received = pl.pallas_call(
        kernel,
        out_shape=(
            sds((tok, width), bf),
            sds((group, tok, 2 * HS), bf),
            sds(packed, bf),
            sds((HS, width), f32),
        ),
        in_specs=[pl.BlockSpec(memory_space=pltpu.HBM)] * len(args),
        out_specs=(VM,) * 4,
        scratch_shapes=[
            vmem((tok, width), bf),
            vmem((tok, width), bf),
            vmem((tok, width), bf),
            vmem((1, tok), jnp.int32),
            vmem((tok, width), bf),
            vmem((HS, width), bf),
            pltpu.SemaphoreType.DMA((6,)),
            vmem((group, tok + half + TAIL, 2 * HS), bf),
            vmem((group, tok + half + TAIL, 2 * HS), bf),
            vmem((length, HS), bf),
            vmem((length + TAIL, HS), bf),
            vmem((length + TAIL, HS), bf),
            vmem((group + 8, tok), f32),
            vmem((group, tok), jnp.int32),
            vmem((1, length), f32),
            vmem((2, HS, QH), f32),
            vmem((2, 8, QH), f32),
            vmem((2, 8, QH), f32),
            vmem((2, length + TAIL, QH), f32),
            vmem((2, group // 2 * per, width), bf),
            vmem((NY * tok, width), bf),
            vmem((2, NY, group // 2 * per, tok), bf),
            vmem((2, NY, group // 2 * per, tok), bf),
            vmem((group, HS, tok), bf),
            vmem((HS, length), bf),
            vmem((HS, length), bf),
            vmem((group, HS, tok), bf),
            vmem((NY, group * per, tok), bf),
            vmem((group * per, NY * tok), bf),
            vmem((group, tok, 2 * HS), bf),
            vmem(packed, bf),
            vmem((HS, length), f32),
            vmem((QB, HS), f32),
            vmem((QB, HS), f32),
            vmem((1, length), f32),
            vmem((group * per, width), bf),
            vmem((group // 2 * per, width), bf),
            vmem((NX, NZH * per, width), bf),
            vmem((NZH * NZL, per // NZL, width), bf),
            vmem((NZH * NZL, per // NZL, width), bf),
            vmem((per // NZL, width), f32),
            vmem((NY, tok, width), bf),
            vmem((NY, tok, width), bf),
            *sems(group),
            *sems(group),
            *sems(group),
            *sems(group),
            *sems(group),
            *sems(NY),
            *sems(2, NY),
            *sems(NY),
            *sems(NY),
            *sems(NZH),
            *sems(NX),
            *sems(1),
            *sems(1),
            *sems(NX),
            *sems(NZH * NZL),
            *sems(NY * NZL),
        ],
        compiler_params=pltpu.CompilerParams(
            vmem_limit_bytes=59 << 20, collective_id=0, has_side_effects=True
        ),
        name="attention_step",
    )(*args)
    output, dq, dk, dv, gw = pl.pallas_call(
        finish_kernel,
        out_shape=(sds((tok, width), bf),) * 4 + (sds((HS, width), f32),),
        in_specs=[VM] * 4,
        out_specs=(VM,) * 5,
        compiler_params=pltpu.CompilerParams(vmem_limit_bytes=60 << 20),
        name="finish",
    )(*received)
    return output[None], dq[None], dk[None], dv[None], gw


def solution(mesh):
    tokens = P("dp", "seq", None)
    return jax.shard_map(
        on_device,
        mesh=mesh,
        in_specs=(tokens, tokens, tokens, P("dp", "seq"), P("seq", None), tokens),
        out_specs=(tokens, tokens, tokens, tokens, P("seq", None)),
        check_vma=False,
    )
```
